1024 devices in a mesh: gx: 32 (over y_lo, z), gy: 16 (over x, core), ha: 2 (over y_hi).
Axes of the slice: x: 8, y: 8 (y_hi: 2, y_lo: 4; y = y_hi * 4 + y_lo), z: 8, core: 2. Of those that a mesh axis runs over, the one named last changes fastest.
Arguments:
- offsets: float32 [3, 64, 32, 4, 128], P(None, 'gx', 'gy', 'ha'), may hold values from 0 to 1
- forces: float32 [3, 64, 32, 4, 128], P(None, 'gx', 'gy', 'ha'), may hold values from -6 to 6
- counts: int32 [64, 32, 4], P('gx', 'gy', 'ha'), may hold values from 16 to 128, as said below
Outputs:
- velocity: float32 [3, 64, 32, 4, 128], P(None, 'gx', 'gy', 'ha')
The draws below stay inside these ranges and needn't reach their ends.
Inputs may be any that keep to these rules, and one draw needn't show every extreme that they name: `counts`: A bin is heavy when its count exceeds 64. The 16 bins that two devices differing only in their ha index hold together include at most 8 heavy bins; in every draw some such pair holds exactly 8, all on one device; some bin holds exactly 128.
All inputs are finite; a program needn't handle non-finite values.
Results may differ from the reference program's by a relative error of at most 0.0003.
Values sent between devices are 32-bit elements; how exact they have to be, the bound alone decides.
A program may use at most 32 MiB of HBM per device.

```python
import math
import jax
import jax.numpy as jnp
from jax import lax

CAP = 128
HALF = 64
BXY = 2
BZ = 2
NBX = 64
NBY = 32
NBZ = 4
NB_DEV = 8


def draw_counts(key, part):
    pair_x = NBX // BXY
    pair_y = NBY // BXY
    per_pair = BXY * BXY * NBZ
    key_score = jax.random.fold_in(key, 11)
    key_many = jax.random.fold_in(key, 12)
    key_light = jax.random.fold_in(key, 13)
    key_heavy = jax.random.fold_in(key, 14)
    raw_score = jax.random.randint(key_score, (pair_x, pair_y, BXY, BXY, NBZ), 0, 1 << 20)
    index_a = jnp.arange(BXY, dtype=jnp.int32)[None, None, :, None, None]
    index_b = jnp.arange(BXY, dtype=jnp.int32)[None, None, None, :, None]
    index_z = jnp.arange(NBZ, dtype=jnp.int32)[None, None, None, None, :]
    local_ids = index_a * (BXY * NBZ) + index_b * NBZ + index_z
    first_pair = (jnp.arange(pair_x, dtype=jnp.int32)[:, None] == 0) & (jnp.arange(pair_y, dtype=jnp.int32)[None, :] == 0)
    lift = jnp.where(first_pair[:, :, None, None, None], index_z // BZ * (1 << 28), 0)
    score = raw_score * per_pair + local_ids + lift
    score = score.reshape(pair_x, pair_y, per_pair)
    ranks = jnp.argsort(jnp.argsort(score, axis=2), axis=2).astype(jnp.int32)
    many_heavy = jax.random.randint(key_many, (pair_x, pair_y), 0, NB_DEV + 1)
    many_heavy = jnp.where(first_pair, NB_DEV, many_heavy)
    heavy_flag = ranks < many_heavy[:, :, None]
    light_count = jax.random.randint(key_light, (pair_x, pair_y, per_pair), CAP // 8, HALF + 1)
    heavy_count = jax.random.randint(key_heavy, (pair_x, pair_y, per_pair), HALF + 1, CAP + 1)
    result = jnp.where(heavy_flag, heavy_count, light_count)
    result = jnp.where(first_pair[:, :, None] & (ranks == 0), CAP, result)
    result = result.reshape(pair_x, pair_y, BXY, BXY, NBZ).transpose(0, 2, 1, 3, 4)
    return result.reshape(NBX, NBY, NBZ).astype(jnp.int32)


def steps_of(stream_key, shape, cuts, least, largest):
    gain, own = 1.0, jax.random.fold_in(stream_key, 6)
    for position, shards_of in cuts:
        draws = jnp.exp(jax.random.uniform(jax.random.fold_in(own, position), (shards_of,), jnp.float32, least / len(cuts), largest / len(cuts)))
        gain = gain * jnp.repeat(draws, shape[position] // shards_of).reshape([-1 if axis == position else 1 for axis in range(len(shape))])
    return gain


def centred(own_key, dims, deviation, limit, pieces=(), kind=jnp.bfloat16):
    entries = jax.random.normal(own_key, dims, jnp.float32) * deviation
    if len(pieces) > 0:
        entries = steps_of(own_key, dims, pieces, -0.22, 0.18) * entries
    return jnp.clip(entries, min=-limit, max=limit).astype(kind)


def setup_inputs(seed: int = 0) -> dict:
    splits = jax.random.split(jax.random.key(seed), 4)
    return {
        "offsets": jnp.clip(1.0 * jax.random.uniform(splits[0], (3, NBX, NBY, NBZ, CAP), jnp.float32) ** steps_of(splits[0], (3, NBX, NBY, NBZ, CAP), ((1, 32), (2, 16), (3, 2)), -0.2, 0.2), 0.0, 1.0),
        "forces": centred(splits[1], (3, NBX, NBY, NBZ, CAP), 1.0, 6.0, ((1, 32), (2, 16), (3, 2)), jnp.float32),
        "counts": draw_counts(jax.random.fold_in(splits[3], 71), 0),
    }


SPLIT_XI = 2.0
SOFT_SQ = 0.01
GAUSS_COEF = 2.0 * SPLIT_XI / math.sqrt(math.pi)
STOKES_NORM = 1.0 / (8.0 * math.pi)

def pair_kernel(targets, row_ids, source_data, capacity):
    n_source = source_data.shape[1]
    flat_ids = jnp.arange(n_source, dtype=jnp.int32)
    neighbour = flat_ids // capacity
    step_x = (neighbour // 9 - 1).astype(jnp.float32)
    step_y = (neighbour // 3 % 3 - 1).astype(jnp.float32)
    step_z = (neighbour % 3 - 1).astype(jnp.float32)
    delta_x = targets[0][:, None] - (source_data[0] + step_x)[None, :]
    delta_y = targets[1][:, None] - (source_data[1] + step_y)[None, :]
    delta_z = targets[2][:, None] - (source_data[2] + step_z)[None, :]
    square = delta_x * delta_x + delta_y * delta_y + delta_z * delta_z + SOFT_SQ
    radius = jnp.sqrt(square)
    tail_erfc = jax.scipy.special.erfc(SPLIT_XI * radius)
    gaussian = jnp.exp(-SPLIT_XI * SPLIT_XI * square)
    coef_c = tail_erfc / radius + GAUSS_COEF * (2.0 * SPLIT_XI * SPLIT_XI * square - 3.0) * gaussian
    coef_d = (tail_erfc / radius + GAUSS_COEF * (1.0 - 2.0 * SPLIT_XI * SPLIT_XI * square) * gaussian) / square
    keep_pair = flat_ids[None, :] != 13 * capacity + row_ids[:, None]
    coef_c = jnp.where(keep_pair, coef_c, 0.0)
    coef_d = jnp.where(keep_pair, coef_d, 0.0)
    force_x = source_data[3][None, :]
    force_y = source_data[4][None, :]
    force_z = source_data[5][None, :]
    along_d = coef_d * (delta_x * force_x + delta_y * force_y + delta_z * force_z)
    vel_x = lax.optimization_barrier(jnp.sum(coef_c * force_x + along_d * delta_x, axis=1))
    vel_y = lax.optimization_barrier(jnp.sum(coef_c * force_y + along_d * delta_y, axis=1))
    vel_z = lax.optimization_barrier(jnp.sum(coef_c * force_z + along_d * delta_z, axis=1))
    return STOKES_NORM * jnp.stack([vel_x, vel_y, vel_z])

def reference(offsets, forces, counts):
    slot_ids = jnp.arange(CAP, dtype=jnp.int32)
    live_mask = (slot_ids[None, None, None, :] < counts[..., None]).astype(jnp.float32)
    packed = jnp.concatenate([offsets, forces * live_mask[None]], axis=0)
    wrapped = jnp.pad(packed, ((0, 0), (1, 1), (1, 1), (1, 1), (0, 0)), mode='wrap')
    zero_index = jnp.zeros((), jnp.int32)

    def one_bin(flat_id):
        flat_id = flat_id.astype(jnp.int32)
        bin_x = (flat_id // (NBY * NBZ)).astype(jnp.int32)
        bin_y = (flat_id // NBZ % NBY).astype(jnp.int32)
        bin_z = (flat_id % NBZ).astype(jnp.int32)
        window = lax.dynamic_slice(wrapped, (zero_index, bin_x, bin_y, bin_z, zero_index), (6, 3, 3, 3, CAP))
        source_data = window.reshape(6, 27 * CAP)
        targets = window[0:3, 1, 1, 1, :]
        return pair_kernel(targets, slot_ids, source_data, CAP)
    result = lax.map(one_bin, jnp.arange(NBX * NBY * NBZ, dtype=jnp.int32))
    result = result.reshape(NBX, NBY, NBZ, 3, CAP).transpose(3, 0, 1, 2, 4)
    return result * live_mask[None]
```

```python
import math

import jax
import jax.numpy as jnp
from jax import lax
from jax.experimental import pallas as pl
from jax.experimental.pallas import tpu as pltpu
from jax.sharding import PartitionSpec as P


GAUSS = 4.0 / math.sqrt(math.pi)
NORM = 1.0 / (8.0 * math.pi)
ERFCX = (-6.605853591129529e-05, 0.2835500330769051, 0.2685154202156198, 0.31675806246707194,
         -0.03963002369445217, 0.48597127806071433, -0.4204782835714706, 0.1053890269858883)
UNIT = 32
BATCH = 8
F32 = jnp.float32
BF16 = jnp.bfloat16


def split3(v):
    a = v.astype(BF16).astype(F32)
    r = v - a
    b = r.astype(BF16).astype(F32)
    return a, b, r - b


def coefs(sq, keep=None):
    rs = lax.rsqrt(sq)
    rad = sq * rs
    z = rad + 1.0
    t = lax.rsqrt(z * z)
    p = ERFCX[7]
    for q in ERFCX[6::-1]:
        p = p * t + q
    e = rs * p
    g = jnp.exp(-4.0 * sq)
    if keep is not None:
        g = jnp.where(keep, g, 0.0)
    a = (8.0 * GAUSS) * sq
    c = g * ((e - 3.0 * GAUSS) + a)
    d = (g * (rs * rs)) * ((e + GAUSS) - a)
    ch = c.astype(BF16)
    cl = (c - ch.astype(F32)).astype(BF16)
    dh = d.astype(BF16)
    dl = (d - dh.astype(F32)).astype(BF16)
    return ch, cl, dh, dl


def near_kernel(reg_ref, out_ref, fa, qf, a_ref, q_ref, b_ref, cc, cd, nq_v, nq_s, lst, sem):
    off = [reg_ref[:, r, :] for r in range(3)]
    frc = [reg_ref[:, 3 + r, :] for r in range(3)]
    cnt = reg_ref[:, 6, :]
    nq = jnp.where(cnt > 32.0, 1, 0) + jnp.where(cnt > 64.0, 1, 0) + jnp.where(cnt > 96.0, 1, 0) + 1
    nq_v[...] = nq.astype(jnp.int32)
    cp = pltpu.make_async_copy(nq_v, nq_s, sem)
    cp.start()
    bid = lax.broadcasted_iota(jnp.int32, (64, 128), 0)
    xi = bid // 16
    yi = (bid // 4) % 4
    zi = bid % 4
    zc = jnp.where(zi == 3, -2, zi - 1)
    pos = [off[0] + (xi - 2).astype(F32), off[1] + (yi - 2).astype(F32), off[2] + zc.astype(F32)]
    nrm = pos[0] * pos[0] + pos[1] * pos[1] + pos[2] * pos[2]
    for a in range(3):
        p = split3(-2.0 * pos[a])
        for i, k in enumerate((0, 0, 0, 1, 1, 2)):
            fa[6 * a + i] = p[k]
    one = jnp.ones((64, 128), F32)
    for i in range(3):
        fa[18 + i] = one
    n3 = split3(nrm)
    for i in range(3):
        fa[21 + i] = n3[i]
    for i in range(24, 32):
        fa[i] = jnp.zeros((64, 128), F32)
    for b in range(3):
        s = split3(frc[b])
        for k in range(3):
            qf[3 * k + b] = s[k]
    for i in range(9, 16):
        qf[i] = jnp.zeros((64, 128), F32)
    w = pos[0] * frc[0] + pos[1] * frc[1] + pos[2] * frc[2]
    qs = frc + [w] + [frc[b] * pos[a] for a in range(3) for b in range(3)] + [w * pos[a] for a in range(3)]
    for i, v in enumerate(qs):
        s = split3(v)
        for k in range(3):
            qf[16 + 16 * k + i] = s[k]

    @pl.loop(0, 64, unroll=4)
    def _(b):
        q = qf[:, b, :].astype(BF16)
        q_ref[b, :, 0:128] = q
        q_ref[b, :, 128:256] = q
        at = fa[:, b, :].T.astype(BF16)
        for u in range(4):
            a_ref[4 * b + u] = at[32 * u:32 * (u + 1)]

    cc[...] = jnp.zeros_like(cc)
    cd[...] = jnp.zeros_like(cd)
    cp.wait()
    rowi = lax.broadcasted_iota(jnp.int32, (128, 128), 0)
    lani = lax.broadcasted_iota(jnp.int32, (128, 128), 1)

    @pl.loop(0, 8)
    def _(o):
        xo = o // 4
        yo = (o // 2) % 2
        ko = o % 2
        ob = (xo + 1) * 16 + (yo + 1) * 4 + ko
        T = reg_ref[ob]
        x = T[0:1] + (xo - 1).astype(F32)
        y = T[1:2] + (yo - 1).astype(F32)
        z = T[2:3] + (ko - 1).astype(F32)
        tp = [x, y, z]
        m3 = split3(x * x + y * y + z * z + 0.01)
        o1 = jnp.ones((1, 128), F32)
        rows = []
        for a in range(3):
            s = split3(tp[a])
            rows += [s[0], s[1], s[2], s[0], s[1], s[0]]
        rows += [m3[0], m3[1], m3[2], o1, o1, o1]
        rows += [jnp.zeros((8, 128), F32)]
        bmat = jnp.concatenate(rows, axis=0).astype(BF16)
        n = jnp.int32(0)
        for j in range(27):
            if j == 13:
                continue
            b = (xo + j // 9) * 16 + (yo + (j // 3) % 3) * 4 + (ko + j % 3 + 3) % 4
            e = b * 512 + j * 4
            for u in range(4):
                lst[n + u] = e * 1 + u * 129
            n = n + nq_s[b, 0]
        for u in range(BATCH):
            lst[n + u] = lst[0]

        aown = jnp.concatenate([a_ref[4 * ob + u] for u in range(4)], axis=0)
        sq = jnp.dot(aown, bmat, preferred_element_type=F32)
        ch, cl, dh, dl = coefs(sq, rowi != lani)
        cc[13, 0:128] = ch
        cc[13, 128:256] = cl
        cd[13, 0:128] = dh
        cd[13, 128:256] = dl

        @pl.loop(0, (n + BATCH - 1) // BATCH)
        def _(it):
            gs = []
            js = []
            for u in range(BATCH):
                v = lst[it * BATCH + u]
                gs.append(v // 128)
                js.append(v % 128)
            am = jnp.concatenate([a_ref[g] for g in gs], axis=0)
            sq = jnp.dot(am, bmat, preferred_element_type=F32)
            ch, cl, dh, dl = coefs(sq)
            for u in range(BATCH):
                j = js[u] // 4
                r = pl.multiple_of((js[u] % 4) * 32, 32)
                s = slice(32 * u, 32 * (u + 1))
                cc[j, pl.ds(r, 32)] = ch[s]
                cc[j, pl.ds(r + 128, 32)] = cl[s]
                cd[j, pl.ds(r, 32)] = dh[s]
                cd[j, pl.ds(r + 128, 32)] = dl[s]

        ac = jnp.zeros((16, 128), F32)
        ad = jnp.zeros((48, 128), F32)
        for j in range(27):
            b = (xo + j // 9) * 16 + (yo + (j // 3) % 3) * 4 + (ko + j % 3 + 3) % 4
            ac = ac + jnp.dot(q_ref[b, 0:16], cc[j], preferred_element_type=F32)
            ad = ad + jnp.dot(q_ref[b, 16:64], cd[j], preferred_element_type=F32)
        cv = (ac[6:9] + ac[3:6]) + ac[0:3]
        dq = (ad[32:48] + ad[16:32]) + ad[0:16]
        live = (lax.broadcasted_iota(jnp.int32, (1, 128), 1).astype(F32) < T[6:7]).astype(F32) * NORM
        xf = (x * dq[0:1] + y * dq[1:2] + z * dq[2:3]) - dq[3:4]
        for a in range(3):
            v = cv[a:a + 1] + tp[a] * xf
            i = 4 + 3 * a
            v = v - ((x * dq[i:i + 1] + y * dq[i + 1:i + 2] + z * dq[i + 2:i + 3]) - dq[13 + a:14 + a])
            out_ref[a, pl.ds(o, 1)] = v * live


def near_call(region):
    return pl.pallas_call(
        near_kernel,
        out_shape=jax.ShapeDtypeStruct((3, 8, 128), F32),
        in_specs=[pl.BlockSpec(memory_space=pltpu.VMEM)],
        out_specs=pl.BlockSpec(memory_space=pltpu.VMEM),
        scratch_shapes=[
            pltpu.VMEM((32, 64, 128), F32),
            pltpu.VMEM((64, 64, 128), F32),
            pltpu.VMEM((256, 32, 32), BF16),
            pltpu.VMEM((64, 64, 256), BF16),
            pltpu.VMEM((32, 128), BF16),
            pltpu.VMEM((27, 256, 128), BF16),
            pltpu.VMEM((27, 256, 128), BF16),
            pltpu.VMEM((64, 128), jnp.int32),
            pltpu.SMEM((64, 128), jnp.int32),
            pltpu.SMEM((160,), jnp.int32),
            pltpu.SemaphoreType.DMA,
        ],
    )(region)


def halo(array, axis, dim):
    n = lax.axis_size(axis)
    up = [(i, (i + 1) % n) for i in range(n)]
    down = [(j, i) for i, j in up]
    last = lax.slice_in_dim(array, 1, 2, axis=dim)
    first = lax.slice_in_dim(array, 0, 1, axis=dim)
    before = lax.ppermute(last, axis, up)
    after = lax.ppermute(first, axis, down)
    return jnp.concatenate([before, array, after], axis=dim)


def on_device(offsets, forces, counts):
    slots = jnp.arange(128, dtype=jnp.int32)
    live = (slots < counts[..., None]).astype(F32)
    rows = jnp.concatenate([offsets, forces * live[None]], axis=0).transpose(1, 2, 3, 0, 4)
    cnt = jnp.broadcast_to(counts.astype(F32)[..., None, None], (2, 2, 2, 2, 128))
    packed = jnp.concatenate([rows, cnt], axis=3)
    ext = halo(halo(packed, "gx", 0), "gy", 1)
    other = lax.ppermute(ext, "ha", [(0, 1), (1, 0)])
    region = jnp.concatenate([ext, other], axis=2).reshape(64, 8, 128)
    return near_call(region).reshape(3, 2, 2, 2, 128)


def solution(mesh):
    spec = P(None, "gx", "gy", "ha", None)
    return jax.shard_map(
        on_device, mesh=mesh, in_specs=(spec, spec, P("gx", "gy", "ha")), out_specs=spec, check_vma=False
    )
```

```python
import math

import jax
import jax.numpy as jnp
from jax import lax
from jax.experimental import pallas as pl
from jax.experimental.pallas import tpu as pltpu
from jax.sharding import PartitionSpec as P


GAUSS = 4.0 / math.sqrt(math.pi)
NORM = 1.0 / (8.0 * math.pi)
ERFCX = (-6.605853591129529e-05, 0.2835500330769051, 0.2685154202156198, 0.31675806246707194,
         -0.03963002369445217, 0.48597127806071433, -0.4204782835714706, 0.1053890269858883)
UNIT = 32
BATCH = 8
F32 = jnp.float32
BF16 = jnp.bfloat16


def split3(v):
    a = v.astype(BF16).astype(F32)
    r = v - a
    b = r.astype(BF16).astype(F32)
    return a, b, r - b


def coefs(sq, keep=None):
    rs = lax.rsqrt(sq)
    rad = sq * rs
    z = rad + 1.0
    t = lax.rsqrt(z * z)
    p = ERFCX[7]
    for q in ERFCX[6::-1]:
        p = p * t + q
    e = rs * p
    g = jnp.exp(-4.0 * sq)
    if keep is not None:
        g = jnp.where(keep, g, 0.0)
    a = (8.0 * GAUSS) * sq
    c = g * ((e - 3.0 * GAUSS) + a)
    d = (g * (rs * rs)) * ((e + GAUSS) - a)
    ch = c.astype(BF16)
    cl = (c - ch.astype(F32)).astype(BF16)
    dh = d.astype(BF16)
    dl = (d - dh.astype(F32)).astype(BF16)
    return ch, cl, dh, dl


def near_kernel(reg_ref, out_ref, fa, qf, a_ref, q_ref, b_ref, cc, cd, nq_v, nq_s, lst, sem):
    off = [reg_ref[:, 4 + r, :] for r in range(3)]
    frc = [reg_ref[:, r, :] for r in range(3)]
    cnt = reg_ref[:, 3, :]
    nq = jnp.where(cnt > 32.0, 1, 0) + jnp.where(cnt > 64.0, 1, 0) + jnp.where(cnt > 96.0, 1, 0) + 1
    nq_v[...] = nq.astype(jnp.int32)
    cp = pltpu.make_async_copy(nq_v, nq_s, sem)
    cp.start()
    bid = lax.broadcasted_iota(jnp.int32, (64, 128), 0)
    xi = bid // 16
    yi = (bid // 4) % 4
    zi = bid % 4
    zc = jnp.where(zi == 3, -2, zi - 1)
    pos = [off[0] + (xi - 2).astype(F32), off[1] + (yi - 2).astype(F32), off[2] + zc.astype(F32)]
    nrm = pos[0] * pos[0] + pos[1] * pos[1] + pos[2] * pos[2]
    for a in range(3):
        p = split3(-2.0 * pos[a])
        for i, k in enumerate((0, 0, 0, 1, 1, 2)):
            fa[6 * a + i] = p[k]
    one = jnp.ones((64, 128), F32)
    for i in range(3):
        fa[18 + i] = one
    n3 = split3(nrm)
    for i in range(3):
        fa[21 + i] = n3[i]
    for i in range(24, 32):
        fa[i] = jnp.zeros((64, 128), F32)
    for b in range(3):
        s = split3(frc[b])
        for k in range(3):
            qf[3 * k + b] = s[k]
    for i in range(9, 16):
        qf[i] = jnp.zeros((64, 128), F32)
    w = pos[0] * frc[0] + pos[1] * frc[1] + pos[2] * frc[2]
    qs = frc + [w] + [frc[b] * pos[a] for a in range(3) for b in range(3)] + [w * pos[a] for a in range(3)]
    for i, v in enumerate(qs):
        s = split3(v)
        for k in range(3):
            qf[16 + 16 * k + i] = s[k]

    @pl.loop(0, 64, unroll=4)
    def _(b):
        q = qf[:, b, :].astype(BF16)
        q_ref[b, :, 0:128] = q
        q_ref[b, :, 128:256] = q
        at = fa[:, b, :].T.astype(BF16)
        for u in range(4):
            a_ref[4 * b + u] = at[32 * u:32 * (u + 1)]

    cc[...] = jnp.zeros_like(cc)
    cd[...] = jnp.zeros_like(cd)
    cp.wait()
    rowi = lax.broadcasted_iota(jnp.int32, (128, 128), 0)
    lani = lax.broadcasted_iota(jnp.int32, (128, 128), 1)

    @pl.loop(0, 8)
    def _(o):
        xo = o // 4
        yo = (o // 2) % 2
        ko = o % 2
        ob = (xo + 1) * 16 + (yo + 1) * 4 + ko
        T = reg_ref[ob]
        x = T[4:5] + (xo - 1).astype(F32)
        y = T[5:6] + (yo - 1).astype(F32)
        z = T[6:7] + (ko - 1).astype(F32)
        tp = [x, y, z]
        m3 = split3(x * x + y * y + z * z + 0.01)
        o1 = jnp.ones((1, 128), F32)
        rows = []
        for a in range(3):
            s = split3(tp[a])
            rows += [s[0], s[1], s[2], s[0], s[1], s[0]]
        rows += [m3[0], m3[1], m3[2], o1, o1, o1]
        rows += [jnp.zeros((8, 128), F32)]
        bmat = jnp.concatenate(rows, axis=0).astype(BF16)
        n = jnp.int32(0)
        for j in range(27):
            if j == 13:
                continue
            b = (xo + j // 9) * 16 + (yo + (j // 3) % 3) * 4 + (ko + j % 3 + 3) % 4
            e = b * 512 + j * 4
            for u in range(4):
                lst[n + u] = e * 1 + u * 129
            n = n + nq_s[b, 0]
        for u in range(BATCH):
            lst[n + u] = lst[0]

        aown = jnp.concatenate([a_ref[4 * ob + u] for u in range(4)], axis=0)
        sq = jnp.dot(aown, bmat, preferred_element_type=F32)
        ch, cl, dh, dl = coefs(sq, rowi != lani)
        cc[13, 0:128] = ch
        cc[13, 128:256] = cl
        cd[13, 0:128] = dh
        cd[13, 128:256] = dl

        @pl.loop(0, (n + BATCH - 1) // BATCH)
        def _(it):
            gs = []
            js = []
            for u in range(BATCH):
                v = lst[it * BATCH + u]
                gs.append(v // 128)
                js.append(v % 128)
            am = jnp.concatenate([a_ref[g] for g in gs], axis=0)
            sq = jnp.dot(am, bmat, preferred_element_type=F32)
            ch, cl, dh, dl = coefs(sq)
            for u in range(BATCH):
                j = js[u] // 4
                r = pl.multiple_of((js[u] % 4) * 32, 32)
                s = slice(32 * u, 32 * (u + 1))
                cc[j, pl.ds(r, 32)] = ch[s]
                cc[j, pl.ds(r + 128, 32)] = cl[s]
                cd[j, pl.ds(r, 32)] = dh[s]
                cd[j, pl.ds(r + 128, 32)] = dl[s]

        ac = jnp.zeros((16, 128), F32)
        ad = jnp.zeros((48, 128), F32)
        for j in range(27):
            b = (xo + j // 9) * 16 + (yo + (j // 3) % 3) * 4 + (ko + j % 3 + 3) % 4
            ac = ac + jnp.dot(q_ref[b, 0:16], cc[j], preferred_element_type=F32)
            ad = ad + jnp.dot(q_ref[b, 16:64], cd[j], preferred_element_type=F32)
        cv = (ac[6:9] + ac[3:6]) + ac[0:3]
        dq = (ad[32:48] + ad[16:32]) + ad[0:16]
        live = (lax.broadcasted_iota(jnp.int32, (1, 128), 1).astype(F32) < T[3:4]).astype(F32) * NORM
        xf = (x * dq[0:1] + y * dq[1:2] + z * dq[2:3]) - dq[3:4]
        for a in range(3):
            v = cv[a:a + 1] + tp[a] * xf
            i = 4 + 3 * a
            v = v - ((x * dq[i:i + 1] + y * dq[i + 1:i + 2] + z * dq[i + 2:i + 3]) - dq[13 + a:14 + a])
            out_ref[a, pl.ds(o, 1)] = v * live


def near_call(region):
    return pl.pallas_call(
        near_kernel,
        out_shape=jax.ShapeDtypeStruct((3, 8, 128), F32),
        in_specs=[pl.BlockSpec(memory_space=pltpu.VMEM)],
        out_specs=pl.BlockSpec(memory_space=pltpu.VMEM),
        scratch_shapes=[
            pltpu.VMEM((32, 64, 128), F32),
            pltpu.VMEM((64, 64, 128), F32),
            pltpu.VMEM((256, 32, 32), BF16),
            pltpu.VMEM((64, 64, 256), BF16),
            pltpu.VMEM((32, 128), BF16),
            pltpu.VMEM((27, 256, 128), BF16),
            pltpu.VMEM((27, 256, 128), BF16),
            pltpu.VMEM((64, 128), jnp.int32),
            pltpu.SMEM((64, 128), jnp.int32),
            pltpu.SMEM((160,), jnp.int32),
            pltpu.SemaphoreType.DMA,
        ],
    )(region)


def halo_kernel(off_ref, frc_ref, cnt_ref, reg_ref, send_ref, send_sems, recv_sems):
    ix = lax.axis_index("gx")
    iy = lax.axis_index("gy")
    ih = lax.axis_index("ha")
    nx = lax.axis_size("gx")
    ny = lax.axis_size("gy")
    peers = []
    for dh in (1, 0):
        for dx in (0, 1, -1):
            for dy in (0, 1, -1):
                if dx or dy or dh:
                    peers.append((dx, dy, dh))

    def at(p):
        return (lax.rem(ix + p[0] + nx, nx), lax.rem(iy + p[1] + ny, ny), lax.rem(ih + p[2], 2))

    barrier = pltpu.get_barrier_semaphore()
    for p in peers:
        pl.semaphore_signal(barrier, inc=1, device_id=at(p), device_id_type=pl.DeviceIdType.MESH)
    lane = lax.broadcasted_iota(jnp.int32, (1, 128), 1)
    for b in range(8):
        n = cnt_ref[b]
        live = (lane < n).astype(F32)
        rows = [frc_ref[r, b:b + 1] * live for r in range(3)] + [jnp.full((1, 128), n, jnp.int32).astype(F32)]
        rows += [off_ref[r, b:b + 1] for r in range(3)] + [jnp.zeros((1, 128), F32)]
        tile = jnp.concatenate(rows, axis=0)
        send_ref[b // 4, (b // 2) % 2, b % 2] = tile
        reg_ref[1 + b // 4, 1 + (b // 2) % 2, b % 2] = tile
    pl.semaphore_wait(barrier, len(peers))
    span = {0: (0, 2), 1: (1, 1), -1: (0, 1)}
    dest = {0: 1, 1: 0, -1: 3}
    copies = []
    for i, p in enumerate(peers):
        (sx, lx), (sy, ly) = span[p[0]], span[p[1]]
        copy = pltpu.make_async_remote_copy(
            src_ref=send_ref.at[pl.ds(sx, lx), pl.ds(sy, ly)],
            dst_ref=reg_ref.at[pl.ds(dest[p[0]], lx), pl.ds(dest[p[1]], ly), pl.ds(2 * p[2], 2)],
            send_sem=send_sems.at[i],
            recv_sem=recv_sems.at[i],
            device_id=at(p),
            device_id_type=pl.DeviceIdType.MESH,
        )
        copy.start()
        copies.append(copy)
    for copy in copies:
        copy.wait_recv()
    for copy in copies:
        copy.wait_send()


def halo_call(offsets, forces, counts):
    return pl.pallas_call(
        halo_kernel,
        out_shape=jax.ShapeDtypeStruct((4, 4, 4, 8, 128), F32),
        in_specs=[
            pl.BlockSpec(memory_space=pltpu.VMEM),
            pl.BlockSpec(memory_space=pltpu.VMEM),
            pl.BlockSpec(memory_space=pltpu.SMEM),
        ],
        out_specs=pl.BlockSpec(memory_space=pltpu.VMEM),
        scratch_shapes=[
            pltpu.VMEM((2, 2, 2, 8, 128), F32),
            pltpu.SemaphoreType.DMA((17,)),
            pltpu.SemaphoreType.DMA((17,)),
        ],
        compiler_params=pltpu.CompilerParams(collective_id=0, has_side_effects=True),
    )(offsets, forces, counts)


def on_device(offsets, forces, counts):
    region = halo_call(offsets.reshape(3, 8, 128), forces.reshape(3, 8, 128), counts.reshape(8))
    return near_call(region.reshape(64, 8, 128)).reshape(3, 2, 2, 2, 128)


def solution(mesh):
    spec = P(None, "gx", "gy", "ha", None)
    return jax.shard_map(
        on_device, mesh=mesh, in_specs=(spec, spec, P("gx", "gy", "ha")), out_specs=spec, check_vma=False
    )
```

```python
import math

import jax
import jax.numpy as jnp
from jax import lax
from jax.experimental import pallas as pl
from jax.experimental.pallas import tpu as pltpu
from jax.sharding import PartitionSpec as P


GAUSS = 4.0 / math.sqrt(math.pi)
NORM = 1.0 / (8.0 * math.pi)
ERFCX = (-6.605853591129529e-05, 0.2835500330769051, 0.2685154202156198, 0.31675806246707194,
         -0.03963002369445217, 0.48597127806071433, -0.4204782835714706, 0.1053890269858883)
BATCH = 16
NJ = 7
TAIL = 22
F32 = jnp.float32
BF16 = jnp.bfloat16


def split3(v):
    a = v.astype(BF16).astype(F32)
    r = v - a
    b = r.astype(BF16).astype(F32)
    return a, b, r - b


def coefs(sq, keep=None):
    rs = lax.rsqrt(sq)
    rad = sq * rs
    z = rad + 1.0
    t = lax.rsqrt(z * z)
    p = ERFCX[7]
    for q in ERFCX[6::-1]:
        p = p * t + q
    e = rs * p
    g = jnp.exp2((-4.0 * math.log2(math.e)) * sq)
    if keep is not None:
        g = jnp.where(keep, g, 0.0)
    a = (8.0 * GAUSS) * sq - 3.0 * GAUSS
    c = g * (e + a)
    d = (g * (rs * rs)) * ((e - a) - 2.0 * GAUSS)
    ch = c.astype(BF16)
    cl = (c - ch.astype(F32)).astype(BF16)
    dh = d.astype(BF16)
    dl = (d - dh.astype(F32)).astype(BF16)
    return ch, cl, dh, dl


def flt(v):
    return float(v) if isinstance(v, int) else v.astype(F32)


def bin_of(o, j):
    return ((o >> 2) + j // 9) * 16 + (((o >> 1) & 1) + (j // 3) % 3) * 4 + (((o & 1) + j % 3 + 3) & 3)


def near_kernel(reg_ref, out_ref, a_ref, q_ref, cc, cd, sqb, acc_c, acc_d, nq_s, lst, tab, cnts):
    sub = lax.broadcasted_iota(jnp.int32, (8, 128), 0)

    def shift_of(b):
        zi = b & 3
        sx = ((b >> 4) - 2).astype(F32)
        sy = (((b >> 2) & 3) - 2).astype(F32)
        sz = jnp.where(zi == 3, -2, zi - 1).astype(F32)
        return sx, sy, sz

    def prep(b):
        tile = reg_ref[b]
        sx, sy, sz = shift_of(b)
        c = tile[3, 0]
        nq_s[b] = (1 + jnp.where(c > 32.0, 1, 0) + jnp.where(c > 64.0, 1, 0) + jnp.where(c > 96.0, 1, 0)).astype(jnp.int32)
        f = tile[0:3]
        x = tile[4:5] + sx
        y = tile[5:6] + sy
        z = tile[6:7] + sz
        n = x * x + y * y + z * z
        m2 = jnp.concatenate([-2.0 * x, -2.0 * y, -2.0 * z, n], axis=0)
        r1, r2, r3 = split3(m2)
        feat = jnp.concatenate([r1, r1, r1, r2, r2, r3, jnp.ones((8, 128), F32)], axis=0)
        at = feat.astype(BF16).astype(F32).T.astype(BF16)
        for u in range(4):
            a_ref[4 * b + u] = at[32 * u:32 * (u + 1)]
        w = x * f[0:1] + y * f[1:2] + z * f[2:3]
        g4 = jnp.concatenate([f, w], axis=0)
        p1 = jnp.concatenate([g4, x * g4], axis=0)
        p2 = jnp.concatenate([y * g4, z * g4], axis=0)
        a3 = split3(p1)
        b3 = split3(p2)
        q = jnp.concatenate([a3[0], a3[1], a3[0], b3[0], a3[1], b3[1], a3[2], b3[2]], axis=0)
        q_ref[b] = q.astype(BF16)

    @pl.loop(0, 16)
    def _(i):
        for k in range(4):
            prep(4 * i + k)

    q_ref[64] = jnp.zeros((64, 128), BF16)
    for i in range(60):
        tab[i] = 64
    rowi = lax.broadcasted_iota(jnp.int32, (128, 128), 0)
    lani = lax.broadcasted_iota(jnp.int32, (128, 128), 1)

    def target(o):
        tile = reg_ref[bin_of(o, 13)]
        x = tile[4:5] + flt((o >> 2) - 1)
        y = tile[5:6] + flt(((o >> 1) & 1) - 1)
        z = tile[6:7] + flt((o & 1) - 1)
        return tile, x, y, z

    def reduce_bins(o1, base, js):
        ac = acc_c[...]
        ad = acc_d[...]
        for j in js:
            q = q_ref[tab[o1 * 64 + j]]
            q2 = jnp.concatenate([q, q], axis=1)
            k = base + 8 * j if isinstance(j, int) else base + 8 * jnp.minimum(j, 26)
            ac = ac + jnp.dot(q2[0:16], cc[pl.ds(k, 8)].reshape(256, 128), preferred_element_type=F32)
            ad = ad + jnp.dot(q2[16:64], cd[pl.ds(k, 8)].reshape(256, 128), preferred_element_type=F32)
        acc_c[...] = ac
        acc_d[...] = ad

    def finish(o):
        tile, x, y, z = target(o)
        tp = [x, y, z]
        cv = acc_c[8:11] + acc_c[0:3]
        dq = (acc_d[32:48] + acc_d[16:32]) + acc_d[0:16]
        live = (lax.broadcasted_iota(jnp.int32, (1, 128), 1).astype(F32) < tile[3:4]).astype(F32) * NORM
        xf = (x * dq[0:1] + y * dq[1:2] + z * dq[2:3]) - dq[3:4]
        for a in range(3):
            i = 4 + 4 * a
            v = cv[a:a + 1] + tp[a] * xf
            v = v - ((x * dq[i:i + 1] + y * dq[i + 1:i + 2] + z * dq[i + 2:i + 3]) - dq[i + 3:i + 4])
            out_ref[a, pl.ds(o, 1)] = v * live

    acc_c[...] = jnp.zeros_like(acc_c)
    acc_d[...] = jnp.zeros_like(acc_d)

    def build(o):
        start = (o & 1) * 160
        n = start
        row = (o + 1) * 64
        corner = (o >> 2) * 16 + ((o >> 1) & 1) * 4
        zs = [((o & 1) + k + 3) & 3 for k in range(3)]
        zb = [corner + z for z in zs]
        for j in range(27):
            b = zb[j % 3] + ((j // 9) * 16 + (j // 3 % 3) * 4)
            tab[row + j] = b
            if j == 13:
                continue
            e = (zb[j % 3] << 10) + (((j // 9) * 16 + (j // 3 % 3) * 4) * 1024 + j * 8)
            for u in range(4):
                lst[n + u] = e + u * 257
            n = n + nq_s[b]
        for j in range(27, 27 + TAIL):
            tab[row + j] = 64
        for u in range(2 * BATCH):
            lst[n + u] = zb[0] << 10
        cnts[o] = n - start

    build(0)

    @pl.loop(0, 8)
    def _(o):
        here = (o & 1) * 216

        @pl.when(o < 2)
        def _():
            blank = jnp.zeros((96, 128), F32).astype(BF16).reshape(3, 32, 128)
            for j in range(27):
                for w in (1, 5):
                    cc[pl.ds(here + 8 * j + w, 3)] = blank
                    cd[pl.ds(here + 8 * j + w, 3)] = blank

        there = 216 - here
        tile, x, y, z = target(o)
        t1, t2, t3 = split3(jnp.concatenate([x, y, z], axis=0))
        m1, m2, m3 = split3(x * x + y * y + z * z + 0.01)
        one = jnp.ones((1, 128), F32)
        zero = jnp.zeros((1, 128), F32)
        bmat = jnp.concatenate(
            [t1, one, t2, zero, t3, zero, t1, one, t2, zero, t1, one, m1, m2, m3, zero, zero, zero, zero, zero], axis=0
        ).astype(BF16)
        n = cnts[o]
        first = (o & 1) * 160
        ob = bin_of(o, 13)
        aown = a_ref[pl.ds(4 * ob, 4)].reshape(128, 32)
        sq = jnp.dot(aown, bmat, preferred_element_type=F32)

        def distances(it):
            am = jnp.concatenate([a_ref[lst[first + it * BATCH + u] >> 8] for u in range(BATCH)], axis=0)
            sqb[it & 1] = jnp.dot(am, bmat, preferred_element_type=F32)

        distances(0)
        pieces = coefs(sq, rowi != lani)
        for u in range(4):
            for k in range(4):
                (cc, cd)[k // 2][here + 104 + u + 4 * (k % 2)] = pieces[k][32 * u:32 * (u + 1)]
        nit = lax.div(n + BATCH - 1, BATCH)
        build(jnp.minimum(o + 1, 7))

        @pl.loop(0, jnp.maximum(nit, -(-27 // NJ)))
        def _(it):
            it2 = jnp.minimum(it, nit - 1)
            pieces = coefs(sqb[it2 & 1])
            reduce_bins(o, there, [it * NJ + i for i in range(NJ)])
            distances(it2 + 1)
            for u in range(BATCH):
                e = here + (lst[first + it2 * BATCH + u] & 255)
                for k in range(4):
                    (cc, cd)[k // 2][e + 4 * (k % 2)] = pieces[k][32 * u:32 * (u + 1)]

        @pl.when(o > 0)
        def _():
            finish(o - 1)
        acc_c[...] = jnp.zeros_like(acc_c)
        acc_d[...] = jnp.zeros_like(acc_d)

    reduce_bins(8, 216, list(range(27)))
    finish(7)


def near_call(region):
    return pl.pallas_call(
        near_kernel,
        out_shape=jax.ShapeDtypeStruct((3, 8, 128), F32),
        in_specs=[pl.BlockSpec(memory_space=pltpu.VMEM)],
        out_specs=pl.BlockSpec(memory_space=pltpu.VMEM),
        scratch_shapes=[
            pltpu.VMEM((256, 32, 32), BF16),
            pltpu.VMEM((65, 64, 128), BF16),
            pltpu.VMEM((432, 32, 128), BF16),
            pltpu.VMEM((432, 32, 128), BF16),
            pltpu.VMEM((2, 32 * BATCH, 128), F32),
            pltpu.VMEM((16, 128), F32),
            pltpu.VMEM((48, 128), F32),
            pltpu.SMEM((64,), jnp.int32),
            pltpu.SMEM((320,), jnp.int32),
            pltpu.SMEM((576,), jnp.int32),
            pltpu.SMEM((8,), jnp.int32),
        ],
    )(region)


def halo_kernel(off_ref, frc_ref, cnt_ref, reg_ref, send_ref, send_sems, recv_sems):
    ix = lax.axis_index("gx")
    iy = lax.axis_index("gy")
    ih = lax.axis_index("ha")
    nx = lax.axis_size("gx")
    ny = lax.axis_size("gy")
    sides = [(dx, dy) for dx in (0, 1, -1) for dy in (0, 1, -1) if dx or dy]
    columns = [(sx, sy) for sx in range(2) for sy in range(2)]

    def at(dx, dy):
        return (lax.rem(ix + dx + nx, nx), lax.rem(iy + dy + ny, ny), ih)

    partner = (ix, iy, 1 - ih)
    barrier = pltpu.get_barrier_semaphore()
    for device in [partner] + [at(*p) for p in sides]:
        pl.semaphore_signal(barrier, inc=1, device_id=device, device_id_type=pl.DeviceIdType.MESH)
    lane = lax.broadcasted_iota(jnp.int32, (1, 128), 1)
    for b in range(8):
        n = cnt_ref[b // 4, (b // 2) % 2, b % 2]
        live = (lane < n).astype(F32)
        rows = [frc_ref[r, b:b + 1] * live for r in range(3)] + [jnp.full((1, 128), n, jnp.int32).astype(F32)]
        rows += [off_ref[r, b:b + 1] for r in range(3)] + [jnp.zeros((1, 128), F32)]
        tile = jnp.concatenate(rows, axis=0)
        send_ref[b // 4, (b // 2) % 2, b % 2] = tile
        reg_ref[1 + b // 4, 1 + (b // 2) % 2, b % 2] = tile
    pl.semaphore_wait(barrier, 9)
    copies = []

    def send(src, dst, device):
        i = len(copies)
        copy = pltpu.make_async_remote_copy(
            src_ref=src,
            dst_ref=dst,
            send_sem=send_sems.at[i],
            recv_sem=recv_sems.at[i],
            device_id=device,
            device_id_type=pl.DeviceIdType.MESH,
        )
        copy.start()
        copies.append(copy)

    for sx, sy in columns:
        send(send_ref.at[sx, sy], reg_ref.at[1 + sx, 1 + sy, pl.ds(2, 2)], partner)
    span = {0: (0, 2), 1: (1, 1), -1: (0, 1)}
    dest = {0: 1, 1: 0, -1: 3}
    for dx, dy in sides:
        (sx, lx), (sy, ly) = span[dx], span[dy]
        send(
            send_ref.at[pl.ds(sx, lx), pl.ds(sy, ly)],
            reg_ref.at[pl.ds(dest[dx], lx), pl.ds(dest[dy], ly), pl.ds(0, 2)],
            at(dx, dy),
        )
    for i, (sx, sy) in enumerate(columns):
        copies[i].wait_recv()
        dx, dy = 2 * sx - 1, 2 * sy - 1
        src = reg_ref.at[1 + sx, 1 + sy, pl.ds(2, 2)]
        for px, py in ((dx, 0), (0, dy), (dx, dy)):
            tx = dest[px] if px else 1 + sx
            ty = dest[py] if py else 1 + sy
            send(src, reg_ref.at[tx, ty, pl.ds(2, 2)], at(px, py))
    for copy in copies[4:]:
        copy.wait_recv()
    for copy in copies:
        copy.wait_send()


def halo_call(offsets, forces, counts):
    return pl.pallas_call(
        halo_kernel,
        out_shape=jax.ShapeDtypeStruct((4, 4, 4, 8, 128), F32),
        in_specs=[
            pl.BlockSpec(memory_space=pltpu.VMEM),
            pl.BlockSpec(memory_space=pltpu.VMEM),
            pl.BlockSpec(memory_space=pltpu.SMEM),
        ],
        out_specs=pl.BlockSpec(memory_space=pltpu.VMEM),
        scratch_shapes=[
            pltpu.VMEM((2, 2, 2, 8, 128), F32),
            pltpu.SemaphoreType.DMA((24,)),
            pltpu.SemaphoreType.DMA((24,)),
        ],
        compiler_params=pltpu.CompilerParams(collective_id=0, has_side_effects=True),
    )(offsets, forces, counts)


def on_device(offsets, forces, counts):
    region = halo_call(offsets.reshape(3, 8, 128), forces.reshape(3, 8, 128), counts)
    return near_call(region.reshape(64, 8, 128)).reshape(3, 2, 2, 2, 128)


def solution(mesh):
    spec = P(None, "gx", "gy", "ha", None)
    return jax.shard_map(
        on_device, mesh=mesh, in_specs=(spec, spec, P("gx", "gy", "ha")), out_specs=spec, check_vma=False
    )
```

```python
import math

import jax
import jax.numpy as jnp
from jax import lax
from jax.experimental import pallas as pl
from jax.experimental.pallas import tpu as pltpu
from jax.sharding import PartitionSpec as P


GAUSS = 4.0 / math.sqrt(math.pi)
NORM = 1.0 / (8.0 * math.pi)
ERFCX = (-6.605853591129529e-05, 0.2835500330769051, 0.2685154202156198, 0.31675806246707194,
         -0.03963002369445217, 0.48597127806071433, -0.4204782835714706, 0.1053890269858883)
F32 = jnp.float32
BF16 = jnp.bfloat16
MESH = pl.DeviceIdType.MESH


def split3(v):
    a = v.astype(BF16).astype(F32)
    r = v - a
    b = r.astype(BF16).astype(F32)
    return a, b, r - b


def coefs(sq, keep=None):
    rs = lax.rsqrt(sq)
    z = sq * rs + 1.0
    t = lax.rsqrt(z * z)
    p = ERFCX[7]
    for q in ERFCX[6::-1]:
        p = p * t + q
    e = rs * p
    g = jnp.exp2((-4.0 * math.log2(math.e)) * sq)
    if keep is not None:
        g = jnp.where(keep, g, 0.0)
    a = (8.0 * GAUSS) * sq - 3.0 * GAUSS
    c = g * (e + a)
    d = (g * (rs * rs)) * ((e - a) - 2.0 * GAUSS)
    ch = c.astype(BF16)
    cl = (c - ch.astype(F32)).astype(BF16)
    dh = d.astype(BF16)
    dl = (d - dh.astype(F32)).astype(BF16)
    return ch, cl, dh, dl


def parts_of(o):
    return lax.div(o, 4), lax.rem(lax.div(o, 2), 2), lax.rem(o, 2)


def pair_own(p):
    o, s = lax.div(p, 8), lax.rem(p, 8)
    return 1 + lax.div(s, 4), 1 + lax.rem(lax.div(s, 2), 2), lax.rem(s, 2), o


def pair_y_near(p):
    o, s = lax.div(p, 4), lax.rem(p, 4)
    return 1 + lax.div(s, 2), 3 * parts_of(o)[1], lax.rem(s, 2), o


def pair_mid_far(p):
    o, s = lax.div(p, 4), lax.rem(p, 4)
    return 1 + lax.div(s, 2), 1 + lax.rem(s, 2), 3 - lax.rem(o, 2), o


def pair_y_far(p):
    o, s = lax.div(p, 2), lax.rem(p, 2)
    return 1 + s, 3 * parts_of(o)[1], 3 - lax.rem(o, 2), o


def pair_x_near(side):
    def pair(p):
        t, s = lax.div(p, 6), lax.rem(p, 6)
        return 3 * side, lax.div(t, 2) + lax.div(s, 2), lax.rem(s, 2), 4 * side + t
    return pair


def pair_x_far(side):
    def pair(p):
        t, s = lax.div(p, 3), lax.rem(p, 3)
        return 3 * side, lax.div(t, 2) + s, 3 - lax.rem(t, 2), 4 * side + t
    return pair


def bins_mid(y0, ystep, z0):
    def new(n):
        return 1 + lax.div(n, 4), y0 + ystep * lax.rem(lax.div(n, 2), 2), z0 + lax.rem(n, 2)
    return new


def bins_side(side, z0):
    def new(n):
        return 3 * side, lax.div(n, 2), z0 + lax.rem(n, 2)
    return new


def near_kernel(off_ref, frc_ref, cnt_ref, out_ref, reg_ref, send_ref, a_ref, q_ref, b_ref, cc, cd, sqb, acc_c, acc_d,
                send_sems, recv_sems):
    ix = lax.axis_index("gx")
    iy = lax.axis_index("gy")
    ih = lax.axis_index("ha")
    nx = lax.axis_size("gx")
    ny = lax.axis_size("gy")
    sides = [(dx, dy) for dx in (0, 1, -1) for dy in (0, 1, -1) if dx or dy]
    columns = [(sx, sy) for sx in range(2) for sy in range(2)]

    def at(dx, dy):
        return (lax.rem(ix + dx + nx, nx), lax.rem(iy + dy + ny, ny), ih)

    partner = (ix, iy, 1 - ih)
    barrier = pltpu.get_barrier_semaphore()
    for device in [partner] + [at(*p) for p in sides]:
        pl.semaphore_signal(barrier, inc=1, device_id=device, device_id_type=MESH)

    lane = lax.broadcasted_iota(jnp.int32, (1, 128), 1)
    one = jnp.ones((1, 128), F32)
    zero = jnp.zeros((1, 128), F32)
    for b in range(8):
        bx, by, bz = b // 4, (b // 2) % 2, b % 2
        n = cnt_ref[bx, by, bz]
        live = (lane < n).astype(F32)
        rows = [frc_ref[r, b:b + 1] * live for r in range(3)] + [live]
        rows += [off_ref[r, b:b + 1] for r in range(3)] + [zero]
        tile = jnp.concatenate(rows, axis=0)
        send_ref[bx, by, bz] = tile
        reg_ref[1 + bx, 1 + by, bz] = tile
        x = tile[4:5] + float(bx - 1)
        y = tile[5:6] + float(by - 1)
        z = tile[6:7] + float(bz - 1)
        t1, t2, t3 = split3(jnp.concatenate([x, y, z], axis=0))
        m1, m2, m3 = split3(x * x + y * y + z * z + 0.01)
        b_ref[b] = jnp.concatenate(
            [t1, one, t2, zero, t3, zero, t1, one, t2, zero, t1, one, m1, m2, m3, zero, zero, zero, zero, zero], axis=0
        ).astype(BF16)
    acc_c[...] = jnp.zeros_like(acc_c)
    acc_d[...] = jnp.zeros_like(acc_d)
    cc[...] = jnp.zeros((4, 256, 128), F32).astype(BF16)
    cd[...] = jnp.zeros((4, 256, 128), F32).astype(BF16)
    sub = lax.broadcasted_iota(jnp.int32, (128, 128), 0)
    diff = lax.broadcasted_iota(jnp.int32, (128, 128), 1) - sub

    def prep(new):
        @pl.loop(0, 2)
        def _(i):
            for k in range(4):
                X, Y, Z = new(4 * i + k)
                b = X * 16 + Y * 4 + Z
                tile = reg_ref[X, Y, Z]
                f = tile[0:3]
                x = tile[4:5] + jnp.asarray(X - 2).astype(F32)
                y = tile[5:6] + jnp.asarray(Y - 2).astype(F32)
                z = tile[6:7] + jnp.asarray(Z - 1 - 4 * lax.div(Z, 3)).astype(F32)
                n = x * x + y * y + z * z
                r1, r2, r3 = split3(jnp.concatenate([-2.0 * x, -2.0 * y, -2.0 * z, n], axis=0))
                feat = jnp.concatenate([r1, r1, r1, r2, r2, r3, jnp.ones((8, 128), F32)], axis=0)
                a_ref[b] = feat.T.astype(BF16)
                w = x * f[0:1] + y * f[1:2] + z * f[2:3]
                g4 = jnp.concatenate([f, w], axis=0)
                a3 = split3(jnp.concatenate([g4, x * g4], axis=0))
                b3 = split3(jnp.concatenate([y * g4, z * g4], axis=0))
                q = jnp.concatenate([a3[0], a3[1], a3[0], b3[0], a3[1], b3[1], a3[2], b3[2]], axis=0)
                q_ref[b] = q.astype(BF16)

    def reduce_pairs(pairs):
        for k, (b, o) in enumerate(pairs):
            q = q_ref[b]
            q2 = jnp.concatenate([q, q], axis=1)
            acc_c[o] = acc_c[o] + jnp.dot(q2[0:16], cc[k], preferred_element_type=F32)
            acc_d[o] = acc_d[o] + jnp.dot(q2[16:64], cd[k], preferred_element_type=F32)

    def distances(pairs):
        for k, (b, o) in enumerate(pairs):
            sqb[k] = jnp.dot(a_ref[b], b_ref[o], preferred_element_type=F32)

    def flat(pair, i):
        out = []
        for k in range(4):
            X, Y, Z, o = pair(jnp.asarray(4 * i + k, jnp.int32))
            out.append((X * 16 + Y * 4 + Z, o))
        return out

    def phase(pair, lo, hi, last, mask=False):
        distances(flat(pair, lo))
        n = hi - lo

        @pl.loop(0, n)
        def _(i):
            began = lax.div(i + n - 1, n)
            now = flat(pair, lo + i - began)
            pending = [(b * began + pb * (1 - began), o * began + po * (1 - began)) for (b, o), (pb, po) in zip(now, last)]
            reduce_pairs(pending)
            for k in range(4):
                keep = None
                if mask:
                    p = 4 * (lo + i) + k
                    same = lax.rem(lax.div(p, 8) - lax.rem(p, 8) + 8, 8)
                    keep = diff != same * 1000
                ch, cl, dh, dl = coefs(sqb[k], keep)
                cc[k, 0:128] = ch
                cc[k, 128:256] = cl
                cd[k, 0:128] = dh
                cd[k, 128:256] = dl
            distances(flat(pair, lo + i + 1 - lax.div(i + 1, n)))

        return [tuple(v) for v in flat(pair, hi - 1)]

    copies = []

    def send(src, dst, device):
        i = len(copies)
        copy = pltpu.make_async_remote_copy(
            src_ref=src, dst_ref=dst, send_sem=send_sems.at[i], recv_sem=recv_sems.at[i],
            device_id=device, device_id_type=MESH,
        )
        copy.start()
        copies.append(copy)

    span = {0: (0, 2), 1: (1, 1), -1: (0, 1)}
    dest = {0: 1, 1: 0, -1: 3}

    prep(bins_mid(1, 1, 0))
    last = flat(pair_own, 0)
    last = phase(pair_own, 0, SPLIT, last, mask=True)

    pl.semaphore_wait(barrier, 9)
    for sx, sy in columns:
        send(send_ref.at[sx, sy], reg_ref.at[1 + sx, 1 + sy, pl.ds(2, 2)], partner)
    for dx, dy in sides:
        (sx, lx), (sy, ly) = span[dx], span[dy]
        send(
            send_ref.at[pl.ds(sx, lx), pl.ds(sy, ly)],
            reg_ref.at[pl.ds(dest[dx], lx), pl.ds(dest[dy], ly), pl.ds(0, 2)],
            at(dx, dy),
        )
    near = {p: 4 + i for i, p in enumerate(sides)}
    if SPLIT < 16:
        last = phase(pair_own, SPLIT, 16, last, mask=True)

    def arrive(which):
        for i in which:
            copies[i].wait_recv()

    arrive([near[0, 1], near[0, -1]])
    prep(bins_mid(0, 3, 0))
    last = phase(pair_y_near, 0, 8, last)
    far = {}
    for i, (sx, sy) in enumerate(columns):
        copies[i].wait_recv()
        dx, dy = 2 * sx - 1, 2 * sy - 1
        src = reg_ref.at[1 + sx, 1 + sy, pl.ds(2, 2)]
        for px, py in ((dx, 0), (0, dy), (dx, dy)):
            tx = dest[px] if px else 1 + sx
            ty = dest[py] if py else 1 + sy
            far.setdefault(px, []).append(len(copies))
            send(src, reg_ref.at[tx, ty, pl.ds(2, 2)], at(px, py))
    prep(bins_mid(1, 1, 2))
    last = phase(pair_mid_far, 0, 8, last)
    arrive([near[-1, dy] for dy in (0, 1, -1)])
    prep(bins_side(1, 0))
    last = phase(pair_x_near(1), 0, 6, last)
    arrive(far[0])
    prep(bins_mid(0, 3, 2))
    last = phase(pair_y_far, 0, 4, last)
    arrive(far[-1])
    prep(bins_side(1, 2))
    last = phase(pair_x_far(1), 0, 3, last)
    arrive([near[1, dy] for dy in (0, 1, -1)])
    prep(bins_side(0, 0))
    last = phase(pair_x_near(0), 0, 6, last)
    arrive(far[1])
    prep(bins_side(0, 2))
    last = phase(pair_x_far(0), 0, 3, last)
    reduce_pairs(last)

    for o in range(8):
        tile = reg_ref[1 + o // 4, 1 + (o // 2) % 2, o % 2]
        x = tile[4:5] + float(o // 4 - 1)
        y = tile[5:6] + float((o // 2) % 2 - 1)
        z = tile[6:7] + float(o % 2 - 1)
        tp = [x, y, z]
        cv = acc_c[o, 8:11] + acc_c[o, 0:3]
        dq = (acc_d[o, 32:48] + acc_d[o, 16:32]) + acc_d[o, 0:16]
        live = tile[3:4] * NORM
        xf = (x * dq[0:1] + y * dq[1:2] + z * dq[2:3]) - dq[3:4]
        for a in range(3):
            i = 4 + 4 * a
            v = cv[a:a + 1] + tp[a] * xf
            v = v - ((x * dq[i:i + 1] + y * dq[i + 1:i + 2] + z * dq[i + 2:i + 3]) - dq[i + 3:i + 4])
            out_ref[a, o:o + 1] = v * live
    for copy in copies:
        copy.wait_send()


SPLIT = 16


def on_device(offsets, forces, counts):
    vel = pl.pallas_call(
        near_kernel,
        out_shape=jax.ShapeDtypeStruct((3, 8, 128), F32),
        in_specs=[
            pl.BlockSpec(memory_space=pltpu.VMEM),
            pl.BlockSpec(memory_space=pltpu.VMEM),
            pl.BlockSpec(memory_space=pltpu.SMEM),
        ],
        out_specs=pl.BlockSpec(memory_space=pltpu.VMEM),
        scratch_shapes=[
            pltpu.VMEM((4, 4, 4, 8, 128), F32),
            pltpu.VMEM((2, 2, 2, 8, 128), F32),
            pltpu.VMEM((64, 128, 32), BF16),
            pltpu.VMEM((64, 64, 128), BF16),
            pltpu.VMEM((8, 32, 128), BF16),
            pltpu.VMEM((4, 256, 128), BF16),
            pltpu.VMEM((4, 256, 128), BF16),
            pltpu.VMEM((4, 128, 128), F32),
            pltpu.VMEM((8, 16, 128), F32),
            pltpu.VMEM((8, 48, 128), F32),
            pltpu.SemaphoreType.DMA((24,)),
            pltpu.SemaphoreType.DMA((24,)),
        ],
        compiler_params=pltpu.CompilerParams(collective_id=0, has_side_effects=True),
    )(offsets.reshape(3, 8, 128), forces.reshape(3, 8, 128), counts)
    return vel.reshape(3, 2, 2, 2, 128)


def solution(mesh):
    spec = P(None, "gx", "gy", "ha", None)
    return jax.shard_map(
        on_device, mesh=mesh, in_specs=(spec, spec, P("gx", "gy", "ha")), out_specs=spec, check_vma=False
    )
```

```python
import math

import jax
import jax.numpy as jnp
from jax import lax
from jax.experimental import pallas as pl
from jax.experimental.pallas import tpu as pltpu
from jax.sharding import PartitionSpec as P


GAUSS = 4.0 / math.sqrt(math.pi)
NORM = 1.0 / (8.0 * math.pi)
ERFCX = (-6.605853591129529e-05, 0.2835500330769051, 0.2685154202156198, 0.31675806246707194,
         -0.03963002369445217, 0.48597127806071433, -0.4204782835714706, 0.1053890269858883)
F32 = jnp.float32
BF16 = jnp.bfloat16
MESH = pl.DeviceIdType.MESH
FORMS = ((1.0, 0.0), (8.0 * GAUSS, -3.0 * GAUSS), (8.0 * GAUSS, -GAUSS), (-4.0 * math.log2(math.e), 0.0))


def split3(v):
    a = v.astype(BF16).astype(F32)
    r = v - a
    b = r.astype(BF16).astype(F32)
    return a, b, r - b


def coefs(sq, ac, ad, arg, keep=None):
    rs = lax.rsqrt(sq)
    z = sq * rs + 1.0
    t = lax.rsqrt(z * z)
    p = ERFCX[7]
    for q in ERFCX[6::-1]:
        p = p * t + q
    e = rs * p
    g = jnp.exp2(arg)
    if keep is not None:
        g = jnp.where(keep, g, 0.0)
    c = g * (e + ac)
    d = (g * (rs * rs)) * (e - ad)
    ch = c.astype(BF16)
    cl = (c - ch.astype(F32)).astype(BF16)
    dh = d.astype(BF16)
    dl = (d - dh.astype(F32)).astype(BF16)
    return ch, cl, dh, dl


def odd(i):
    return i - 2 * lax.shift_right_logical(i, 1)


def pair_own(i, k):
    return 16 + 16 * odd(i) + (1 + k // 2) * 4 + k % 2, lax.shift_right_logical(i, 1)


def pair_y_near(i, k):
    return (1 + k // 2) * 16 + 12 * odd(lax.shift_right_logical(i, 1)) + k % 2, i


def pair_mid_far(i, k):
    return (1 + k // 2) * 16 + (1 + k % 2) * 4 + 3 - odd(i), i


def pair_y_far(i, k):
    return (1 + k % 2) * 16 + 12 * odd(i) + 3 - k // 2, 2 * i + k // 2


def pair_x_near(side):
    def pair(i, k):
        y = lax.shift_right_logical(11 * i, 5)
        return 48 * side + (i - 2 * y) * 4 + k % 2, 4 * side + 2 * y + k // 2
    return pair


def pair_x_far(side):
    def pair(i, k):
        return 48 * side + (k // 2 + i) * 4 + 3 - k % 2, jnp.int32(0) + 4 * side + k
    return pair


def bins_mid(y0, ystep, z0):
    def new(n):
        return 1 + lax.div(n, 4), y0 + ystep * lax.rem(lax.div(n, 2), 2), z0 + lax.rem(n, 2)
    return new


def bins_side(side, z0):
    def new(n):
        return 3 * side, lax.div(n, 2), z0 + lax.rem(n, 2)
    return new


def near_kernel(off_ref, frc_ref, cnt_ref, out_ref, reg_ref, send_ref, a_ref, q_ref, b_ref, cc, cd, sqb, acc_c, acc_d,
                send_sems, recv_sems):
    ix = lax.axis_index("gx")
    iy = lax.axis_index("gy")
    ih = lax.axis_index("ha")
    nx = lax.axis_size("gx")
    ny = lax.axis_size("gy")
    sides = [(dx, dy) for dx in (0, 1, -1) for dy in (0, 1, -1) if dx or dy]
    columns = [(sx, sy) for sx in range(2) for sy in range(2)]

    def at(dx, dy):
        return (lax.rem(ix + dx + nx, nx), lax.rem(iy + dy + ny, ny), ih)

    partner = (ix, iy, 1 - ih)
    barrier = pltpu.get_barrier_semaphore()
    for device in [partner] + [at(*p) for p in sides]:
        pl.semaphore_signal(barrier, inc=1, device_id=device, device_id_type=MESH)

    lane = lax.broadcasted_iota(jnp.int32, (1, 128), 1)
    one = jnp.ones((1, 128), F32)
    zero = jnp.zeros((1, 128), F32)
    for b in range(8):
        bx, by, bz = b // 4, (b // 2) % 2, b % 2
        n = cnt_ref[bx, by, bz]
        live = (lane < n).astype(F32)
        rows = [frc_ref[r, b:b + 1] * live for r in range(3)] + [live]
        rows += [off_ref[r, b:b + 1] for r in range(3)] + [zero]
        tile = jnp.concatenate(rows, axis=0)
        send_ref[bx, by, bz] = tile
        reg_ref[1 + bx, 1 + by, bz] = tile
        x = tile[4:5] + float(bx - 1)
        y = tile[5:6] + float(by - 1)
        z = tile[6:7] + float(bz - 1)
        m = x * x + y * y + z * z + 0.01
        for k, (scale, extra) in enumerate(FORMS):
            t1, t2, t3 = split3(scale * jnp.concatenate([x, y, z, one], axis=0))
            m1, m2, m3 = split3(scale * m + extra)
            b_ref[b, :, 128 * k:128 * (k + 1)] = jnp.concatenate(
                [t1, t2, t3, t1, t2, t1, m1, m2, m3, zero, zero, zero, zero, zero], axis=0
            ).astype(BF16)
    acc_c[...] = jnp.zeros_like(acc_c)
    acc_d[...] = jnp.zeros_like(acc_d)
    cc[...] = jnp.zeros((4, 256, 128), F32).astype(BF16)
    cd[...] = jnp.zeros((4, 256, 128), F32).astype(BF16)
    sub = lax.broadcasted_iota(jnp.int32, (128, 128), 0)
    diff = lax.broadcasted_iota(jnp.int32, (128, 128), 1) - sub

    def prep(new):
        @pl.loop(0, 2)
        def _(i):
            for k in range(4):
                X, Y, Z = new(4 * i + k)
                b = X * 16 + Y * 4 + Z
                tile = reg_ref[X, Y, Z]
                f = tile[0:3]
                x = tile[4:5] + jnp.asarray(X - 2).astype(F32)
                y = tile[5:6] + jnp.asarray(Y - 2).astype(F32)
                z = tile[6:7] + jnp.asarray(Z - 1 - 4 * lax.div(Z, 3)).astype(F32)
                n = x * x + y * y + z * z
                r1, r2, r3 = split3(jnp.concatenate([-2.0 * x, -2.0 * y, -2.0 * z, n], axis=0))
                feat = jnp.concatenate([r1, r1, r1, r2, r2, r3, jnp.ones((8, 128), F32)], axis=0)
                a_ref[b] = feat.T.astype(BF16)
                w = x * f[0:1] + y * f[1:2] + z * f[2:3]
                g4 = jnp.concatenate([f, w], axis=0)
                a3 = split3(jnp.concatenate([g4, x * g4], axis=0))
                b3 = split3(jnp.concatenate([y * g4, z * g4], axis=0))
                q = jnp.concatenate([a3[0], a3[1], a3[0], b3[0], a3[1], b3[1], a3[2], b3[2]], axis=0)
                q_ref[b] = q.astype(BF16)

    def reduce_pairs(pairs, first=0):
        for k, (b, o) in enumerate(pairs, first):
            q = q_ref[b]
            q2 = jnp.concatenate([q, q], axis=1)
            acc_c[o] = acc_c[o] + jnp.dot(q2[0:16], cc[k], preferred_element_type=F32)
            acc_d[o] = acc_d[o] + jnp.dot(q2[16:64], cd[k], preferred_element_type=F32)

    def distances(pairs, first=0):
        for k, (b, o) in enumerate(pairs, first):
            sqb[k] = jnp.dot(a_ref[b], b_ref[o], preferred_element_type=F32)

    def flat(pair, i):
        return [pair(jnp.asarray(i, jnp.int32), k) for k in range(4)]

    def phase(pair, n, last, mask=False):
        distances(flat(pair, 0))

        @pl.loop(0, n)
        def _(i):
            began = lax.div(i + n - 1, n)
            now = flat(pair, i - began)
            pending = [(pb + began * (b - pb), po + began * (o - po)) for (b, o), (pb, po) in zip(now, last)]
            later = flat(pair, i + 1 - lax.div(i + 1, n))
            for k in range(4):
                keep = None
                if mask:
                    off = 4 * odd(i) + k - lax.shift_right_logical(i, 1)
                    keep = diff != off * off * 1000
                v = sqb[k]
                ch, cl, dh, dl = coefs(v[:, 0:128], v[:, 128:256], v[:, 256:384], v[:, 384:512], keep)
                distances([later[k]], k)
                reduce_pairs([pending[k]], k)
                cc[k, 0:128] = ch
                cc[k, 128:256] = cl
                cd[k, 0:128] = dh
                cd[k, 128:256] = dl

        return flat(pair, n - 1)

    copies = []

    def send(src, dst, device):
        i = len(copies)
        copy = pltpu.make_async_remote_copy(
            src_ref=src, dst_ref=dst, send_sem=send_sems.at[i], recv_sem=recv_sems.at[i],
            device_id=device, device_id_type=MESH,
        )
        copy.start()
        copies.append(copy)

    span = {0: (0, 2), 1: (1, 1), -1: (0, 1)}
    dest = {0: 1, 1: 0, -1: 3}

    prep(bins_mid(1, 1, 0))
    last = flat(pair_own, 0)
    last = phase(pair_own, 16, last, mask=True)

    pl.semaphore_wait(barrier, 9)
    for sx, sy in columns:
        send(send_ref.at[sx, sy], reg_ref.at[1 + sx, 1 + sy, pl.ds(2, 2)], partner)
    for dx, dy in sides:
        (sx, lx), (sy, ly) = span[dx], span[dy]
        send(
            send_ref.at[pl.ds(sx, lx), pl.ds(sy, ly)],
            reg_ref.at[pl.ds(dest[dx], lx), pl.ds(dest[dy], ly), pl.ds(0, 2)],
            at(dx, dy),
        )
    near = {p: 4 + i for i, p in enumerate(sides)}

    def arrive(which):
        for i in which:
            copies[i].wait_recv()

    arrive([near[0, 1], near[0, -1]])
    prep(bins_mid(0, 3, 0))
    last = phase(pair_y_near, 8, last)
    far = {}
    for i, (sx, sy) in enumerate(columns):
        copies[i].wait_recv()
        dx, dy = 2 * sx - 1, 2 * sy - 1
        src = reg_ref.at[1 + sx, 1 + sy, pl.ds(2, 2)]
        for px, py in ((dx, 0), (0, dy), (dx, dy)):
            tx = dest[px] if px else 1 + sx
            ty = dest[py] if py else 1 + sy
            far.setdefault(px, []).append(len(copies))
            send(src, reg_ref.at[tx, ty, pl.ds(2, 2)], at(px, py))
    prep(bins_mid(1, 1, 2))
    last = phase(pair_mid_far, 8, last)
    arrive([near[-1, dy] for dy in (0, 1, -1)])
    prep(bins_side(1, 0))
    last = phase(pair_x_near(1), 6, last)
    arrive(far[0])
    prep(bins_mid(0, 3, 2))
    last = phase(pair_y_far, 4, last)
    arrive(far[-1])
    prep(bins_side(1, 2))
    last = phase(pair_x_far(1), 3, last)
    arrive([near[1, dy] for dy in (0, 1, -1)])
    prep(bins_side(0, 0))
    last = phase(pair_x_near(0), 6, last)
    arrive(far[1])
    prep(bins_side(0, 2))
    last = phase(pair_x_far(0), 3, last)
    reduce_pairs(last)

    for o in range(8):
        tile = reg_ref[1 + o // 4, 1 + (o // 2) % 2, o % 2]
        x = tile[4:5] + float(o // 4 - 1)
        y = tile[5:6] + float((o // 2) % 2 - 1)
        z = tile[6:7] + float(o % 2 - 1)
        tp = [x, y, z]
        cv = acc_c[o, 8:11] + acc_c[o, 0:3]
        dq = (acc_d[o, 32:48] + acc_d[o, 16:32]) + acc_d[o, 0:16]
        live = tile[3:4] * NORM
        xf = (x * dq[0:1] + y * dq[1:2] + z * dq[2:3]) - dq[3:4]
        for a in range(3):
            i = 4 + 4 * a
            v = cv[a:a + 1] + tp[a] * xf
            v = v - ((x * dq[i:i + 1] + y * dq[i + 1:i + 2] + z * dq[i + 2:i + 3]) - dq[i + 3:i + 4])
            out_ref[a, o:o + 1] = v * live
    for copy in copies:
        copy.wait_send()


def on_device(offsets, forces, counts):
    vel = pl.pallas_call(
        near_kernel,
        out_shape=jax.ShapeDtypeStruct((3, 8, 128), F32),
        in_specs=[
            pl.BlockSpec(memory_space=pltpu.VMEM),
            pl.BlockSpec(memory_space=pltpu.VMEM),
            pl.BlockSpec(memory_space=pltpu.SMEM),
        ],
        out_specs=pl.BlockSpec(memory_space=pltpu.VMEM),
        scratch_shapes=[
            pltpu.VMEM((4, 4, 4, 8, 128), F32),
            pltpu.VMEM((2, 2, 2, 8, 128), F32),
            pltpu.VMEM((64, 128, 32), BF16),
            pltpu.VMEM((64, 64, 128), BF16),
            pltpu.VMEM((8, 32, 512), BF16),
            pltpu.VMEM((4, 256, 128), BF16),
            pltpu.VMEM((4, 256, 128), BF16),
            pltpu.VMEM((4, 128, 512), F32),
            pltpu.VMEM((8, 16, 128), F32),
            pltpu.VMEM((8, 48, 128), F32),
            pltpu.SemaphoreType.DMA((24,)),
            pltpu.SemaphoreType.DMA((24,)),
        ],
        compiler_params=pltpu.CompilerParams(collective_id=0, has_side_effects=True),
    )(offsets.reshape(3, 8, 128), forces.reshape(3, 8, 128), counts)
    return vel.reshape(3, 2, 2, 2, 128)


def solution(mesh):
    spec = P(None, "gx", "gy", "ha", None)
    return jax.shard_map(
        on_device, mesh=mesh, in_specs=(spec, spec, P("gx", "gy", "ha")), out_specs=spec, check_vma=False
    )
```

```python
import math

import jax
import jax.numpy as jnp
from jax import lax
from jax.experimental import pallas as pl
from jax.experimental.pallas import tpu as pltpu
from jax.sharding import PartitionSpec as P


GAUSS = 4.0 / math.sqrt(math.pi)
NORM = 1.0 / (8.0 * math.pi)
ERFCX = (-6.605853591129529e-05, 0.2835500330769051, 0.2685154202156198, 0.31675806246707194,
         -0.03963002369445217, 0.48597127806071433, -0.4204782835714706, 0.1053890269858883)
F32 = jnp.float32
BF16 = jnp.bfloat16
MESH = pl.DeviceIdType.MESH
FORMS = ((1.0, 0.0), (8.0 * GAUSS, -3.0 * GAUSS), (8.0 * GAUSS, -GAUSS), (-4.0 * math.log2(math.e), 0.0))


def split3(v):
    a = v.astype(BF16).astype(F32)
    r = v - a
    b = r.astype(BF16).astype(F32)
    return a, b, r - b


def coefs(sq, ac, ad, arg, keep=None):
    rs = lax.rsqrt(sq)
    z = sq * rs + 1.0
    t = lax.rsqrt(z * z)
    p = ERFCX[7]
    for q in ERFCX[6::-1]:
        p = p * t + q
    e = rs * p
    g = jnp.exp2(arg)
    if keep is not None:
        g = jnp.where(keep, g, 0.0)
    c = g * (e + ac)
    d = (g * (rs * rs)) * (e - ad)
    ch = c.astype(BF16)
    cl = (c - ch.astype(F32)).astype(BF16)
    dh = d.astype(BF16)
    dl = (d - dh.astype(F32)).astype(BF16)
    return ch, cl, dh, dl


def odd(i):
    return i - 2 * lax.shift_right_logical(i, 1)


def pair_own(i, k):
    return 16 + 16 * odd(i) + (1 + k // 2) * 4 + k % 2, lax.shift_right_logical(i, 1)


def pair_y_near(i, k):
    return (1 + k // 2) * 16 + 12 * odd(lax.shift_right_logical(i, 1)) + k % 2, i


def pair_mid_far(i, k):
    return (1 + k // 2) * 16 + (1 + k % 2) * 4 + 3 - odd(i), i


def pair_y_far(i, k):
    return (1 + k % 2) * 16 + 12 * odd(i) + 3 - k // 2, 2 * i + k // 2


def pair_x_near(side):
    def pair(i, k):
        y = lax.shift_right_logical(11 * i, 5)
        return 48 * side + (i - 2 * y) * 4 + k % 2, 4 * side + 2 * y + k // 2
    return pair


def pair_x_far(side):
    def pair(i, k):
        return 48 * side + (k // 2 + i) * 4 + 3 - k % 2, jnp.int32(0) + 4 * side + k
    return pair


def bins_mid(y0, ystep, z0):
    def new(n):
        return 1 + n // 4, y0 + ystep * ((n // 2) % 2), z0 + n % 2
    return new


def bins_side(side, z0):
    def new(n):
        return 3 * side, n // 2, z0 + n % 2
    return new


def machinery(tile_of, a_ref, q_ref, b_ref, cc, cd, sqb, acc_c, acc_d):
    sub = lax.broadcasted_iota(jnp.int32, (128, 128), 0)
    diff = lax.broadcasted_iota(jnp.int32, (128, 128), 1) - sub
    one = jnp.ones((1, 128), F32)
    zero = jnp.zeros((1, 128), F32)
    cc[...] = jnp.zeros((4, 256, 128), F32).astype(BF16)
    cd[...] = jnp.zeros((4, 256, 128), F32).astype(BF16)

    def target(o):
        tile = tile_of(1 + o // 4, 1 + (o // 2) % 2, o % 2)
        x = tile[4:5] + float(o // 4 - 1)
        y = tile[5:6] + float((o // 2) % 2 - 1)
        z = tile[6:7] + float(o % 2 - 1)
        return tile, x, y, z

    def targets():
        for o in range(8):
            tile, x, y, z = target(o)
            m = x * x + y * y + z * z + 0.01
            for k, (scale, extra) in enumerate(FORMS):
                t1, t2, t3 = split3(scale * jnp.concatenate([x, y, z, one], axis=0))
                m1, m2, m3 = split3(scale * m + extra)
                b_ref[o, :, 128 * k:128 * (k + 1)] = jnp.concatenate(
                    [t1, t2, t3, t1, t2, t1, m1, m2, m3, zero, zero, zero, zero, zero], axis=0
                ).astype(BF16)

    def prep(new):
        for k in range(8):
            X, Y, Z = new(k)
            b = X * 16 + Y * 4 + Z
            tile = tile_of(X, Y, Z)
            f = tile[0:3]
            x = tile[4:5] + float(X - 2)
            y = tile[5:6] + float(Y - 2)
            z = tile[6:7] + float(Z - 1 - 4 * (Z // 3))
            n = x * x + y * y + z * z
            r1, r2, r3 = split3(jnp.concatenate([-2.0 * x, -2.0 * y, -2.0 * z, n], axis=0))
            feat = jnp.concatenate([r1, r1, r1, r2, r2, r3, jnp.ones((8, 128), F32)], axis=0)
            a_ref[b] = feat.T.astype(BF16)
            w = x * f[0:1] + y * f[1:2] + z * f[2:3]
            g4 = jnp.concatenate([f, w], axis=0)
            a3 = split3(jnp.concatenate([g4, x * g4], axis=0))
            b3 = split3(jnp.concatenate([y * g4, z * g4], axis=0))
            q = jnp.concatenate([a3[0], a3[1], a3[0], b3[0], a3[1], b3[1], a3[2], b3[2]], axis=0)
            q_ref[b] = q.astype(BF16)

    def reduce_pairs(pairs, first=0):
        for k, (b, o) in enumerate(pairs, first):
            q = q_ref[b]
            q2 = jnp.concatenate([q, q], axis=1)
            acc_c[o] = acc_c[o] + jnp.dot(q2[0:16], cc[k], preferred_element_type=F32)
            acc_d[o] = acc_d[o] + jnp.dot(q2[16:64], cd[k], preferred_element_type=F32)

    def distances(pairs, first=0):
        for k, (b, o) in enumerate(pairs, first):
            sqb[k] = jnp.dot(a_ref[b], b_ref[o], preferred_element_type=F32)

    def flat(pair, i):
        return [pair(jnp.asarray(i, jnp.int32), k) for k in range(4)]

    def phase(pair, n, last, mask=False, opening=True, following=None):
        if opening:
            distances(flat(pair, 0))

        @pl.loop(0, n)
        def _(i):
            began = lax.div(i + n - 1, n)
            now = flat(pair, i - began)
            pending = [(pb + began * (b - pb), po + began * (o - po)) for (b, o), (pb, po) in zip(now, last)]
            ended = lax.div(i + 1, n)
            later = flat(pair, i + 1 - ended)
            if following is not None:
                first = flat(following, 0)
                later = [(b + ended * (nb - b), o + ended * (no - o)) for (b, o), (nb, no) in zip(later, first)]
            for k in range(4):
                keep = None
                if mask:
                    off = 4 * odd(i) + k - lax.shift_right_logical(i, 1)
                    keep = diff != off * off * 1000
                v = sqb[k]
                ch, cl, dh, dl = coefs(v[:, 0:128], v[:, 128:256], v[:, 256:384], v[:, 384:512], keep)
                distances([later[k]], k)
                reduce_pairs([pending[k]], k)
                cc[k, 0:128] = ch
                cc[k, 128:256] = cl
                cd[k, 0:128] = dh
                cd[k, 128:256] = dl

        return flat(pair, n - 1)

    return target, targets, prep, reduce_pairs, flat, phase


def own_kernel(off_ref, frc_ref, cnt_ref, mid_ref, acc_c, acc_d, send_ref, a_ref, q_ref, b_ref, cc, cd, sqb, send_sems, recv_sems):
    ix = lax.axis_index("gx")
    iy = lax.axis_index("gy")
    ih = lax.axis_index("ha")
    ny = lax.axis_size("gy")
    partner = (ix, iy, 1 - ih)
    beside = {dy: (ix, lax.rem(iy + dy + ny, ny), ih) for dy in (1, -1)}
    barrier = pltpu.get_barrier_semaphore()
    for device in (partner, beside[1], beside[-1]):
        pl.semaphore_signal(barrier, inc=1, device_id=device, device_id_type=MESH)

    lane = lax.broadcasted_iota(jnp.int32, (1, 128), 1)
    for b in range(8):
        bx, by, bz = b // 4, (b // 2) % 2, b % 2
        live = (lane < cnt_ref[bx, by, bz]).astype(F32)
        rows = [frc_ref[r, b:b + 1] * live for r in range(3)] + [live]
        rows += [off_ref[r, b:b + 1] for r in range(3)] + [jnp.zeros((1, 128), F32)]
        tile = jnp.concatenate(rows, axis=0)
        send_ref[bx, by, bz] = tile
        mid_ref[bx, 1 + by, bz] = tile
    acc_c[...] = jnp.zeros_like(acc_c)
    acc_d[...] = jnp.zeros_like(acc_d)
    target, targets, prep, reduce_pairs, flat, phase = machinery(
        lambda X, Y, Z: mid_ref[X - 1, Y, Z], a_ref, q_ref, b_ref, cc, cd, sqb, acc_c, acc_d
    )
    copies = []

    def send(src, dst, device):
        i = len(copies)
        copy = pltpu.make_async_remote_copy(
            src_ref=src, dst_ref=dst, send_sem=send_sems.at[i], recv_sem=recv_sems.at[i],
            device_id=device, device_id_type=MESH,
        )
        copy.start()
        copies.append(copy)

    targets()
    prep(bins_mid(1, 1, 0))
    pl.semaphore_wait(barrier, 3)
    columns = [(sx, sy) for sx in range(2) for sy in range(2)]
    for sx, sy in columns:
        send(send_ref.at[sx, sy], mid_ref.at[sx, 1 + sy, pl.ds(2, 2)], partner)
    for dy in (1, -1):
        for sx in range(2):
            send(send_ref.at[sx, (1 + dy) // 2], mid_ref.at[sx, (3 - 3 * dy) // 2, pl.ds(0, 2)], beside[dy])
    last = flat(pair_own, 0)
    last = phase(pair_own, 16, last, mask=True)
    for i, (sx, sy) in enumerate(columns):
        copies[i].wait_recv()
        dy = 2 * sy - 1
        send(mid_ref.at[sx, 1 + sy, pl.ds(2, 2)], mid_ref.at[sx, (3 - 3 * dy) // 2, pl.ds(2, 2)], beside[dy])
    reduce_pairs(last)
    for copy in copies[4:]:
        copy.wait_recv()
    for copy in copies:
        copy.wait_send()


def near_kernel(mid_ref, acc_c_in, acc_d_in, out_ref, side_ref, acc_c, acc_d, a_ref, q_ref, b_ref, cc, cd, sqb, send_sems, recv_sems):
    ix = lax.axis_index("gx")
    iy = lax.axis_index("gy")
    ih = lax.axis_index("ha")
    nx = lax.axis_size("gx")
    up = (lax.rem(ix + 1, nx), iy, ih)
    down = (lax.rem(ix + nx - 1, nx), iy, ih)
    barrier = pltpu.get_barrier_semaphore()
    for device in (up, down):
        pl.semaphore_signal(barrier, inc=1, device_id=device, device_id_type=MESH)

    def copy_of(i, plane, side, device):
        return pltpu.make_async_remote_copy(
            src_ref=mid_ref.at[plane], dst_ref=side_ref.at[side], send_sem=send_sems.at[i], recv_sem=recv_sems.at[i],
            device_id=device, device_id_type=MESH,
        )

    to_up = copy_of(0, 1, 0, up)
    to_down = copy_of(1, 0, 1, down)

    def exchange():
        pl.semaphore_wait(barrier, 2)
        to_up.start()
        to_down.start()

    first = lax.rem(ix, 8)

    @pl.when(first > 0)
    def _():
        exchange()

    acc_c[...] = acc_c_in[...]
    acc_d[...] = acc_d_in[...]

    def tile_of(X, Y, Z):
        return mid_ref[X - 1, Y, Z] if X in (1, 2) else side_ref[X // 3, Y, Z]

    target, targets, prep, reduce_pairs, flat, phase = machinery(
        tile_of, a_ref, q_ref, b_ref, cc, cd, sqb, acc_c, acc_d
    )
    targets()
    for new in (bins_mid(0, 3, 0), bins_mid(1, 1, 2), bins_mid(0, 3, 2)):
        prep(new)
    last = phase(pair_y_near, 8, flat(pair_y_near, 0), following=pair_mid_far)
    last = phase(pair_mid_far, 8, last, opening=False, following=pair_y_far)
    last = phase(pair_y_far, 4, last, opening=False)
    to_down.wait_recv()
    prep(bins_side(1, 0))
    prep(bins_side(1, 2))
    last = phase(pair_x_near(1), 6, last, following=pair_x_far(1))
    last = phase(pair_x_far(1), 3, last, opening=False)

    @pl.when(first == 0)
    def _():
        exchange()

    to_up.wait_recv()
    prep(bins_side(0, 0))
    prep(bins_side(0, 2))
    last = phase(pair_x_near(0), 6, last, following=pair_x_far(0))
    last = phase(pair_x_far(0), 3, last, opening=False)
    reduce_pairs(last)

    for o in range(8):
        tile, x, y, z = target(o)
        tp = [x, y, z]
        cv = acc_c[o, 8:11] + acc_c[o, 0:3]
        dq = (acc_d[o, 32:48] + acc_d[o, 16:32]) + acc_d[o, 0:16]
        live = tile[3:4] * NORM
        xf = (x * dq[0:1] + y * dq[1:2] + z * dq[2:3]) - dq[3:4]
        for a in range(3):
            i = 4 + 4 * a
            v = cv[a:a + 1] + tp[a] * xf
            v = v - ((x * dq[i:i + 1] + y * dq[i + 1:i + 2] + z * dq[i + 2:i + 3]) - dq[i + 3:i + 4])
            out_ref[a, o:o + 1] = v * live
    to_up.wait_send()
    to_down.wait_send()


WORK = [
    pltpu.VMEM((64, 128, 32), BF16),
    pltpu.VMEM((64, 64, 128), BF16),
    pltpu.VMEM((8, 32, 512), BF16),
    pltpu.VMEM((4, 256, 128), BF16),
    pltpu.VMEM((4, 256, 128), BF16),
    pltpu.VMEM((4, 128, 512), F32),
]
SUMS = [(8, 16, 128), (8, 48, 128)]


def on_device(offsets, forces, counts):
    vmem = pl.BlockSpec(memory_space=pltpu.VMEM)
    mid, sum_c, sum_d = pl.pallas_call(
        own_kernel,
        out_shape=[jax.ShapeDtypeStruct(s, F32) for s in [(2, 4, 4, 8, 128)] + SUMS],
        in_specs=[vmem, vmem, pl.BlockSpec(memory_space=pltpu.SMEM)],
        out_specs=[vmem] * 3,
        scratch_shapes=[pltpu.VMEM((2, 2, 2, 8, 128), F32)] + WORK + [pltpu.SemaphoreType.DMA((12,))] * 2,
        compiler_params=pltpu.CompilerParams(collective_id=0, has_side_effects=True),
    )(offsets.reshape(3, 8, 128), forces.reshape(3, 8, 128), counts)
    vel = pl.pallas_call(
        near_kernel,
        out_shape=jax.ShapeDtypeStruct((3, 8, 128), F32),
        in_specs=[vmem] * 3,
        out_specs=vmem,
        scratch_shapes=[pltpu.VMEM((2, 4, 4, 8, 128), F32)] + [pltpu.VMEM(s, F32) for s in SUMS] + WORK
        + [pltpu.SemaphoreType.DMA((2,))] * 2,
        compiler_params=pltpu.CompilerParams(collective_id=1, has_side_effects=True),
    )(mid, sum_c, sum_d)
    return vel.reshape(3, 2, 2, 2, 128)


def solution(mesh):
    spec = P(None, "gx", "gy", "ha", None)
    return jax.shard_map(
        on_device, mesh=mesh, in_specs=(spec, spec, P("gx", "gy", "ha")), out_specs=spec, check_vma=False
    )
```

```python
import math

import jax
import jax.numpy as jnp
from jax import lax
from jax.experimental import pallas as pl
from jax.experimental.pallas import tpu as pltpu
from jax.sharding import PartitionSpec as P


GAUSS = 4.0 / math.sqrt(math.pi)
NORM = 1.0 / (8.0 * math.pi)
ERFCX = (-6.605853591129529e-05, 0.2835500330769051, 0.2685154202156198, 0.31675806246707194,
         -0.03963002369445217, 0.48597127806071433, -0.4204782835714706, 0.1053890269858883)
F32 = jnp.float32
BF16 = jnp.bfloat16
MESH = pl.DeviceIdType.MESH
FORMS = ((1.0, 0.0), (8.0 * GAUSS, -3.0 * GAUSS), (8.0 * GAUSS, -GAUSS), (-4.0 * math.log2(math.e), 0.0))


def split3(v):
    a = v.astype(BF16).astype(F32)
    r = v - a
    b = r.astype(BF16).astype(F32)
    return a, b, r - b


def coefs(sq, ac, ad, arg, keep=None):
    rs = lax.rsqrt(sq)
    z = sq * rs + 1.0
    t = lax.rsqrt(z * z)
    p = ERFCX[7]
    for q in ERFCX[6::-1]:
        p = p * t + q
    e = rs * p
    g = jnp.exp2(arg)
    if keep is not None:
        g = jnp.where(keep, g, 0.0)
    c = g * (e + ac)
    d = (g * (rs * rs)) * (e - ad)
    ch = c.astype(BF16)
    cl = (c - ch.astype(F32)).astype(BF16)
    dh = d.astype(BF16)
    dl = (d - dh.astype(F32)).astype(BF16)
    return ch, cl, dh, dl


def odd(i):
    return i - 2 * lax.shift_right_logical(i, 1)


def pair_own(i, k):
    return 16 + 16 * odd(i) + (1 + k // 2) * 4 + k % 2, lax.shift_right_logical(i, 1)


def pair_y_near(i, k):
    return (1 + k // 2) * 16 + 12 * odd(lax.shift_right_logical(i, 1)) + k % 2, i


def pair_mid_far(i, k):
    return (1 + k // 2) * 16 + (1 + k % 2) * 4 + 3 - odd(i), i


def pair_y_far(i, k):
    return (1 + k % 2) * 16 + 12 * odd(i) + 3 - k // 2, 2 * i + k // 2


def pair_x_near(side):
    def pair(i, k):
        y = lax.shift_right_logical(11 * i, 5)
        return 48 * side + (i - 2 * y) * 4 + k % 2, 4 * side + 2 * y + k // 2
    return pair


def pair_x_far(side):
    def pair(i, k):
        return 48 * side + (k // 2 + i) * 4 + 3 - k % 2, jnp.int32(0) + 4 * side + k
    return pair


def bins_mid(y0, ystep, z0):
    def new(n):
        return 1 + n // 4, y0 + ystep * ((n // 2) % 2), z0 + n % 2
    return new


def bins_side(side, z0):
    def new(n):
        return 3 * side, n // 2, z0 + n % 2
    return new


def machinery(tile_of, a_ref, q_ref, b_ref, cc, cd, sqb, acc_c, acc_d):
    sub = lax.broadcasted_iota(jnp.int32, (128, 128), 0)
    diff = lax.broadcasted_iota(jnp.int32, (128, 128), 1) - sub
    one = jnp.ones((1, 128), F32)
    zero = jnp.zeros((1, 128), F32)
    cc[...] = jnp.zeros((4, 256, 128), F32).astype(BF16)
    cd[...] = jnp.zeros((4, 256, 128), F32).astype(BF16)

    def target(o):
        tile = tile_of(1 + o // 4, 1 + (o // 2) % 2, o % 2)
        x = tile[4:5] + float(o // 4 - 1)
        y = tile[5:6] + float((o // 2) % 2 - 1)
        z = tile[6:7] + float(o % 2 - 1)
        return tile, x, y, z

    def targets():
        for o in range(8):
            tile, x, y, z = target(o)
            m = x * x + y * y + z * z + 0.01
            for k, (scale, extra) in enumerate(FORMS):
                t1, t2, t3 = split3(scale * jnp.concatenate([x, y, z, one], axis=0))
                m1, m2, m3 = split3(scale * m + extra)
                b_ref[o, :, 128 * k:128 * (k + 1)] = jnp.concatenate(
                    [t1, t2, t3, t1, t2, t1, m1, m2, m3, zero, zero, zero, zero, zero], axis=0
                ).astype(BF16)

    def prep(new):
        for k in range(8):
            X, Y, Z = new(k)
            b = X * 16 + Y * 4 + Z
            tile = tile_of(X, Y, Z)
            f = tile[0:3]
            x = tile[4:5] + float(X - 2)
            y = tile[5:6] + float(Y - 2)
            z = tile[6:7] + float(Z - 1 - 4 * (Z // 3))
            n = x * x + y * y + z * z
            r1, r2, r3 = split3(jnp.concatenate([-2.0 * x, -2.0 * y, -2.0 * z, n], axis=0))
            feat = jnp.concatenate([r1, r1, r1, r2, r2, r3, jnp.ones((8, 128), F32)], axis=0)
            a_ref[b] = feat.T.astype(BF16)
            w = x * f[0:1] + y * f[1:2] + z * f[2:3]
            g4 = jnp.concatenate([f, w], axis=0)
            a3 = split3(jnp.concatenate([g4, x * g4], axis=0))
            b3 = split3(jnp.concatenate([y * g4, z * g4], axis=0))
            q = jnp.concatenate([a3[0], a3[1], a3[0], b3[0], a3[1], b3[1], a3[2], b3[2]], axis=0)
            q_ref[b] = q.astype(BF16)

    def reduce_pairs(pairs, first=0):
        for k, (b, o) in enumerate(pairs, first):
            q = q_ref[b]
            q2 = jnp.concatenate([q, q], axis=1)
            acc_c[o] = acc_c[o] + jnp.dot(q2[0:16], cc[k], preferred_element_type=F32)
            acc_d[o] = acc_d[o] + jnp.dot(q2[16:64], cd[k], preferred_element_type=F32)

    def distances(pairs, first=0):
        for k, (b, o) in enumerate(pairs, first):
            sqb[k] = jnp.dot(a_ref[b], b_ref[o], preferred_element_type=F32)

    def flat(pair, i):
        return [pair(jnp.asarray(i, jnp.int32), k) for k in range(4)]

    def phase(pair, n, last, mask=False, opening=True, following=None, start=0):
        if opening:
            distances(flat(pair, start))

        @pl.loop(0, n)
        def _(i):
            began = lax.div(i + n - 1, n)
            now = flat(pair, start + i - began)
            pending = [(pb + began * (b - pb), po + began * (o - po)) for (b, o), (pb, po) in zip(now, last)]
            ended = lax.div(i + 1, n)
            later = flat(pair, start + i + 1 - ended)
            if following is not None:
                first = flat(following, 0)
                later = [(b + ended * (nb - b), o + ended * (no - o)) for (b, o), (nb, no) in zip(later, first)]
            for k in range(4):
                keep = None
                if mask:
                    off = 4 * odd(start + i) + k - lax.shift_right_logical(start + i, 1)
                    keep = diff != off * off * 1000
                v = sqb[k]
                ch, cl, dh, dl = coefs(v[:, 0:128], v[:, 128:256], v[:, 256:384], v[:, 384:512], keep)
                distances([later[k]], k)
                reduce_pairs([pending[k]], k)
                cc[k, 0:128] = ch
                cc[k, 128:256] = cl
                cd[k, 0:128] = dh
                cd[k, 128:256] = dl

        return flat(pair, start + n - 1)

    return target, targets, prep, reduce_pairs, flat, phase


def own_kernel(off_ref, frc_ref, cnt_ref, mid_ref, acc_c, acc_d, send_ref, a_ref, q_ref, b_ref, cc, cd, sqb, send_sems, recv_sems):
    ix = lax.axis_index("gx")
    iy = lax.axis_index("gy")
    ih = lax.axis_index("ha")
    ny = lax.axis_size("gy")
    partner = (ix, iy, 1 - ih)
    beside = {dy: (ix, lax.rem(iy + dy + ny, ny), ih) for dy in (1, -1)}
    barrier = pltpu.get_barrier_semaphore()
    for device in (partner, beside[1], beside[-1]):
        pl.semaphore_signal(barrier, inc=1, device_id=device, device_id_type=MESH)

    lane = lax.broadcasted_iota(jnp.int32, (1, 128), 1)
    for b in range(8):
        bx, by, bz = b // 4, (b // 2) % 2, b % 2
        live = (lane < cnt_ref[bx, by, bz]).astype(F32)
        rows = [frc_ref[r, b:b + 1] * live for r in range(3)] + [live]
        rows += [off_ref[r, b:b + 1] for r in range(3)] + [jnp.zeros((1, 128), F32)]
        tile = jnp.concatenate(rows, axis=0)
        send_ref[bx, by, bz] = tile
        mid_ref[bx, 1 + by, bz] = tile
    acc_c[...] = jnp.zeros_like(acc_c)
    acc_d[...] = jnp.zeros_like(acc_d)
    target, targets, prep, reduce_pairs, flat, phase = machinery(
        lambda X, Y, Z: mid_ref[X - 1, Y, Z], a_ref, q_ref, b_ref, cc, cd, sqb, acc_c, acc_d
    )
    copies = []

    def send(src, dst, device):
        i = len(copies)
        copy = pltpu.make_async_remote_copy(
            src_ref=src, dst_ref=dst, send_sem=send_sems.at[i], recv_sem=recv_sems.at[i],
            device_id=device, device_id_type=MESH,
        )
        copy.start()
        copies.append(copy)

    targets()
    prep(bins_mid(1, 1, 0))
    pl.semaphore_wait(barrier, 3)
    columns = [(sx, sy) for sx in range(2) for sy in range(2)]
    for sx, sy in columns:
        send(send_ref.at[sx, sy], mid_ref.at[sx, 1 + sy, pl.ds(2, 2)], partner)
    for dy in (1, -1):
        for sx in range(2):
            send(send_ref.at[sx, (1 + dy) // 2], mid_ref.at[sx, (3 - 3 * dy) // 2, pl.ds(0, 2)], beside[dy])
    last = flat(pair_own, 0)
    last = phase(pair_own, 10, last, mask=True)
    for i, (sx, sy) in enumerate(columns):
        copies[i].wait_recv()
        dy = 2 * sy - 1
        send(mid_ref.at[sx, 1 + sy, pl.ds(2, 2)], mid_ref.at[sx, (3 - 3 * dy) // 2, pl.ds(2, 2)], beside[dy])
    last = phase(pair_own, 6, last, mask=True, start=10)
    reduce_pairs(last)
    for copy in copies[4:]:
        copy.wait_recv()
    for copy in copies:
        copy.wait_send()


def near_kernel(mid_ref, acc_c_in, acc_d_in, out_ref, side_ref, acc_c, acc_d, a_ref, q_ref, b_ref, cc, cd, sqb, send_sems, recv_sems):
    ix = lax.axis_index("gx")
    iy = lax.axis_index("gy")
    ih = lax.axis_index("ha")
    nx = lax.axis_size("gx")
    up = (lax.rem(ix + 1, nx), iy, ih)
    down = (lax.rem(ix + nx - 1, nx), iy, ih)
    barrier = pltpu.get_barrier_semaphore()
    for device in (up, down):
        pl.semaphore_signal(barrier, inc=1, device_id=device, device_id_type=MESH)

    def copy_of(i, plane, side, device):
        return pltpu.make_async_remote_copy(
            src_ref=mid_ref.at[plane], dst_ref=side_ref.at[side], send_sem=send_sems.at[i], recv_sem=recv_sems.at[i],
            device_id=device, device_id_type=MESH,
        )

    to_up = copy_of(0, 1, 0, up)
    to_down = copy_of(1, 0, 1, down)

    def exchange():
        pl.semaphore_wait(barrier, 2)
        to_up.start()
        to_down.start()

    first = lax.rem(ix, 8)

    @pl.when(first > 0)
    def _():
        exchange()

    acc_c[...] = acc_c_in[...]
    acc_d[...] = acc_d_in[...]

    def tile_of(X, Y, Z):
        return mid_ref[X - 1, Y, Z] if X in (1, 2) else side_ref[X // 3, Y, Z]

    target, targets, prep, reduce_pairs, flat, phase = machinery(
        tile_of, a_ref, q_ref, b_ref, cc, cd, sqb, acc_c, acc_d
    )
    targets()
    for new in (bins_mid(0, 3, 0), bins_mid(1, 1, 2), bins_mid(0, 3, 2)):
        prep(new)
    last = phase(pair_y_near, 8, flat(pair_y_near, 0), following=pair_mid_far)
    last = phase(pair_mid_far, 8, last, opening=False, following=pair_y_far)

    @pl.when(first == 0)
    def _():
        exchange()

    last = phase(pair_y_far, 4, last, opening=False)
    to_down.wait_recv()
    prep(bins_side(1, 0))
    prep(bins_side(1, 2))
    last = phase(pair_x_near(1), 6, last, following=pair_x_far(1))
    last = phase(pair_x_far(1), 3, last, opening=False)

    to_up.wait_recv()
    prep(bins_side(0, 0))
    prep(bins_side(0, 2))
    last = phase(pair_x_near(0), 6, last, following=pair_x_far(0))
    last = phase(pair_x_far(0), 3, last, opening=False)
    reduce_pairs(last)

    for o in range(8):
        tile, x, y, z = target(o)
        tp = [x, y, z]
        cv = acc_c[o, 8:11] + acc_c[o, 0:3]
        dq = (acc_d[o, 32:48] + acc_d[o, 16:32]) + acc_d[o, 0:16]
        live = tile[3:4] * NORM
        xf = (x * dq[0:1] + y * dq[1:2] + z * dq[2:3]) - dq[3:4]
        for a in range(3):
            i = 4 + 4 * a
            v = cv[a:a + 1] + tp[a] * xf
            v = v - ((x * dq[i:i + 1] + y * dq[i + 1:i + 2] + z * dq[i + 2:i + 3]) - dq[i + 3:i + 4])
            out_ref[a, o:o + 1] = v * live
    to_up.wait_send()
    to_down.wait_send()


WORK = [
    pltpu.VMEM((64, 128, 32), BF16),
    pltpu.VMEM((64, 64, 128), BF16),
    pltpu.VMEM((8, 32, 512), BF16),
    pltpu.VMEM((4, 256, 128), BF16),
    pltpu.VMEM((4, 256, 128), BF16),
    pltpu.VMEM((4, 128, 512), F32),
]
SUMS = [(8, 16, 128), (8, 48, 128)]


def on_device(offsets, forces, counts):
    vmem = pl.BlockSpec(memory_space=pltpu.VMEM)
    mid, sum_c, sum_d = pl.pallas_call(
        own_kernel,
        out_shape=[jax.ShapeDtypeStruct(s, F32) for s in [(2, 4, 4, 8, 128)] + SUMS],
        in_specs=[vmem, vmem, pl.BlockSpec(memory_space=pltpu.SMEM)],
        out_specs=[vmem] * 3,
        scratch_shapes=[pltpu.VMEM((2, 2, 2, 8, 128), F32)] + WORK + [pltpu.SemaphoreType.DMA((12,))] * 2,
        compiler_params=pltpu.CompilerParams(collective_id=0, has_side_effects=True),
    )(offsets.reshape(3, 8, 128), forces.reshape(3, 8, 128), counts)
    vel = pl.pallas_call(
        near_kernel,
        out_shape=jax.ShapeDtypeStruct((3, 8, 128), F32),
        in_specs=[vmem] * 3,
        out_specs=vmem,
        scratch_shapes=[pltpu.VMEM((2, 4, 4, 8, 128), F32)] + [pltpu.VMEM(s, F32) for s in SUMS] + WORK
        + [pltpu.SemaphoreType.DMA((2,))] * 2,
        compiler_params=pltpu.CompilerParams(collective_id=1, has_side_effects=True),
    )(mid, sum_c, sum_d)
    return vel.reshape(3, 2, 2, 2, 128)


def solution(mesh):
    spec = P(None, "gx", "gy", "ha", None)
    return jax.shard_map(
        on_device, mesh=mesh, in_specs=(spec, spec, P("gx", "gy", "ha")), out_specs=spec, check_vma=False
    )
```

```python
import math

import jax
import jax.numpy as jnp
from jax import lax
from jax.experimental import pallas as pl
from jax.experimental.pallas import tpu as pltpu
from jax.sharding import PartitionSpec as P


GAUSS = 4.0 / math.sqrt(math.pi)
NORM = 1.0 / (8.0 * math.pi)
ERFCX = (-6.605853591129529e-05, 0.2835500330769051, 0.2685154202156198, 0.31675806246707194,
         -0.03963002369445217, 0.48597127806071433, -0.4204782835714706, 0.1053890269858883)
F32 = jnp.float32
BF16 = jnp.bfloat16
MESH = pl.DeviceIdType.MESH
FORMS = ((1.0, 0.0), (8.0 * GAUSS, -3.0 * GAUSS), (8.0 * GAUSS, -GAUSS), (-4.0 * math.log2(math.e), 0.0))


def split3(v):
    a = v.astype(BF16).astype(F32)
    r = v - a
    b = r.astype(BF16).astype(F32)
    return a, b, r - b


def coefs(sq, ac, ad, arg, keep=None):
    rs = lax.rsqrt(sq)
    z = sq * rs + 1.0
    t = lax.rsqrt(z * z)
    p = ERFCX[7]
    for q in ERFCX[6::-1]:
        p = p * t + q
    e = rs * p
    g = jnp.exp2(arg)
    if keep is not None:
        g = jnp.where(keep, g, 0.0)
    c = g * (e + ac)
    d = (g * (rs * rs)) * (e - ad)
    ch = c.astype(BF16)
    cl = (c - ch.astype(F32)).astype(BF16)
    dh = d.astype(BF16)
    dl = (d - dh.astype(F32)).astype(BF16)
    return ch, cl, dh, dl


def odd(i):
    return i - 2 * lax.shift_right_logical(i, 1)


def pair_own(i, k):
    return 16 + 16 * odd(i) + (1 + k // 2) * 4 + k % 2, lax.shift_right_logical(i, 1)


def pair_y_near(i, k):
    return (1 + k // 2) * 16 + 12 * odd(lax.shift_right_logical(i, 1)) + k % 2, i


def pair_mid_far(i, k):
    return (1 + k // 2) * 16 + (1 + k % 2) * 4 + 3 - odd(i), i


def pair_y_far(i, k):
    return (1 + k % 2) * 16 + 12 * odd(i) + 3 - k // 2, 2 * i + k // 2


def pair_x_near(side):
    def pair(i, k):
        y = lax.shift_right_logical(11 * i, 5)
        return 48 * side + (i - 2 * y) * 4 + k % 2, 4 * side + 2 * y + k // 2
    return pair


def pair_x_far(side):
    def pair(i, k):
        return 48 * side + (k // 2 + i) * 4 + 3 - k % 2, jnp.int32(0) + 4 * side + k
    return pair


def bins_mid(y0, ystep, z0):
    def new(n):
        return 1 + n // 4, y0 + ystep * ((n // 2) % 2), z0 + n % 2
    return new


def bins_side(side, z0):
    def new(n):
        return 3 * side, n // 2, z0 + n % 2
    return new


def machinery(tile_of, a_ref, q_ref, b_ref, cc, cd, sqb, acc_c, acc_d):
    sub = lax.broadcasted_iota(jnp.int32, (128, 128), 0)
    diff = lax.broadcasted_iota(jnp.int32, (128, 128), 1) - sub
    one = jnp.ones((1, 128), F32)
    zero = jnp.zeros((1, 128), F32)
    cc[...] = jnp.zeros((4, 256, 128), F32).astype(BF16)
    cd[...] = jnp.zeros((4, 256, 128), F32).astype(BF16)
    q_ref[64] = jnp.zeros((64, 128), F32).astype(BF16)

    def target(o):
        tile = tile_of(1 + o // 4, 1 + (o // 2) % 2, o % 2)
        x = tile[4:5] + float(o // 4 - 1)
        y = tile[5:6] + float((o // 2) % 2 - 1)
        z = tile[6:7] + float(o % 2 - 1)
        return tile, x, y, z

    def targets():
        for o in range(8):
            tile, x, y, z = target(o)
            m = x * x + y * y + z * z + 0.01
            for k, (scale, extra) in enumerate(FORMS):
                t1, t2, t3 = split3(scale * jnp.concatenate([x, y, z, one], axis=0))
                m1, m2, m3 = split3(scale * m + extra)
                b_ref[o, :, 128 * k:128 * (k + 1)] = jnp.concatenate(
                    [t1, t2, t3, t1, t2, t1, m1, m2, m3, zero, zero, zero, zero, zero], axis=0
                ).astype(BF16)

    def prep(new):
        for k in range(8):
            X, Y, Z = new(k)
            b = X * 16 + Y * 4 + Z
            tile = tile_of(X, Y, Z)
            f = tile[0:3]
            x = tile[4:5] + float(X - 2)
            y = tile[5:6] + float(Y - 2)
            z = tile[6:7] + float(Z - 1 - 4 * (Z // 3))
            n = x * x + y * y + z * z
            r1, r2, r3 = split3(jnp.concatenate([-2.0 * x, -2.0 * y, -2.0 * z, n], axis=0))
            feat = jnp.concatenate([r1, r1, r1, r2, r2, r3, jnp.ones((8, 128), F32)], axis=0)
            a_ref[b] = feat.T.astype(BF16)
            w = x * f[0:1] + y * f[1:2] + z * f[2:3]
            g4 = jnp.concatenate([f, w], axis=0)
            a3 = split3(jnp.concatenate([g4, x * g4], axis=0))
            b3 = split3(jnp.concatenate([y * g4, z * g4], axis=0))
            q = jnp.concatenate([a3[0], a3[1], a3[0], b3[0], a3[1], b3[1], a3[2], b3[2]], axis=0)
            q_ref[b] = q.astype(BF16)

    def reduce_pairs(pairs, first=0):
        for k, (b, o) in enumerate(pairs, first):
            q = q_ref[b]
            q2 = jnp.concatenate([q, q], axis=1)
            acc_c[o] = acc_c[o] + jnp.dot(q2[0:16], cc[k], preferred_element_type=F32)
            acc_d[o] = acc_d[o] + jnp.dot(q2[16:64], cd[k], preferred_element_type=F32)

    def distances(pairs, first=0):
        for k, (b, o) in enumerate(pairs, first):
            sqb[k] = jnp.dot(a_ref[b], b_ref[o], preferred_element_type=F32)

    def flat(pair, i):
        return [pair(jnp.asarray(i, jnp.int32), k) for k in range(4)]

    def phase(pair, n, last, mask=False, opening=True, following=None, start=0):
        if opening:
            distances(flat(pair, start))

        @pl.loop(0, n)
        def _(i):
            began = lax.div(i + n - 1, n)
            now = flat(pair, start + i - began)
            pending = [(pb + began * (b - pb), po + began * (o - po)) for (b, o), (pb, po) in zip(now, last)]
            ended = lax.div(i + 1, n)
            later = flat(pair, start + i + 1 - ended)
            if following is not None:
                first = flat(following, 0)
                later = [(b + ended * (nb - b), o + ended * (no - o)) for (b, o), (nb, no) in zip(later, first)]
            for k in range(4):
                keep = None
                if mask:
                    off = 4 * odd(start + i) + k - lax.shift_right_logical(start + i, 1)
                    keep = diff != off * off * 1000
                v = sqb[k]
                ch, cl, dh, dl = coefs(v[:, 0:128], v[:, 128:256], v[:, 256:384], v[:, 384:512], keep)
                distances([later[k]], k)
                reduce_pairs([pending[k]], k)
                cc[k, 0:128] = ch
                cc[k, 128:256] = cl
                cd[k, 0:128] = dh
                cd[k, 128:256] = dl

        return flat(pair, start + n - 1)

    return target, targets, prep, reduce_pairs, flat, phase


def lateness(ix, iy, ny):
    return lax.rem(ix, 8) * 2 + lax.div(ny - iy, ny)


def own_kernel(off_ref, frc_ref, cnt_ref, mid_ref, acc_c, acc_d, send_ref, a_ref, q_ref, b_ref, cc, cd, sqb, send_sems, recv_sems):
    ix = lax.axis_index("gx")
    iy = lax.axis_index("gy")
    ih = lax.axis_index("ha")
    ny = lax.axis_size("gy")
    partner = (ix, iy, 1 - ih)
    beside = {dy: (ix, lax.rem(iy + dy + ny, ny), ih) for dy in (1, -1)}
    barrier = pltpu.get_barrier_semaphore()
    for device in (partner, beside[1], beside[-1]):
        pl.semaphore_signal(barrier, inc=1, device_id=device, device_id_type=MESH)

    lane = lax.broadcasted_iota(jnp.int32, (1, 128), 1)
    for b in range(8):
        bx, by, bz = b // 4, (b // 2) % 2, b % 2
        live = (lane < cnt_ref[bx, by, bz]).astype(F32)
        rows = [frc_ref[r, b:b + 1] * live for r in range(3)] + [live]
        rows += [off_ref[r, b:b + 1] for r in range(3)] + [jnp.zeros((1, 128), F32)]
        tile = jnp.concatenate(rows, axis=0)
        send_ref[bx, by, bz] = tile
        mid_ref[bx, 1 + by, bz] = tile
    acc_c[...] = jnp.zeros_like(acc_c)
    acc_d[...] = jnp.zeros_like(acc_d)
    target, targets, prep, reduce_pairs, flat, phase = machinery(
        lambda X, Y, Z: mid_ref[X - 1, Y, Z], a_ref, q_ref, b_ref, cc, cd, sqb, acc_c, acc_d
    )
    copies = []

    def send(src, dst, device):
        i = len(copies)
        copy = pltpu.make_async_remote_copy(
            src_ref=src, dst_ref=dst, send_sem=send_sems.at[i], recv_sem=recv_sems.at[i],
            device_id=device, device_id_type=MESH,
        )
        copy.start()
        copies.append(copy)

    targets()
    prep(bins_mid(1, 1, 0))
    late = lateness(ix, iy, ny)

    @pl.when(late == 0)
    def _():
        reduce_pairs(phase(pair_own, 16, NONE, mask=True))

    pl.semaphore_wait(barrier, 3)
    columns = [(sx, sy) for sx in range(2) for sy in range(2)]
    for sx, sy in columns:
        send(send_ref.at[sx, sy], mid_ref.at[sx, 1 + sy, pl.ds(2, 2)], partner)
    for dy in (1, -1):
        for sx in range(2):
            send(send_ref.at[sx, (1 + dy) // 2], mid_ref.at[sx, (3 - 3 * dy) // 2, pl.ds(0, 2)], beside[dy])

    @pl.when(late > 0)
    def _():
        reduce_pairs(phase(pair_own, 10, NONE, mask=True))

    for i, (sx, sy) in enumerate(columns):
        copies[i].wait_recv()
        dy = 2 * sy - 1
        send(mid_ref.at[sx, 1 + sy, pl.ds(2, 2)], mid_ref.at[sx, (3 - 3 * dy) // 2, pl.ds(2, 2)], beside[dy])

    @pl.when(late > 0)
    def _():
        reduce_pairs(phase(pair_own, 6, NONE, mask=True, start=10))

    @pl.when(late == 0)
    def _():
        prep(bins_mid(1, 1, 2))
        reduce_pairs(phase(pair_mid_far, 8, NONE))

    for copy in copies[4:]:
        copy.wait_recv()
    for copy in copies:
        copy.wait_send()


def near_kernel(mid_ref, acc_c_in, acc_d_in, out_ref, side_ref, acc_c, acc_d, a_ref, q_ref, b_ref, cc, cd, sqb, send_sems, recv_sems):
    ix = lax.axis_index("gx")
    iy = lax.axis_index("gy")
    ih = lax.axis_index("ha")
    nx = lax.axis_size("gx")
    ny = lax.axis_size("gy")
    late = lateness(ix, iy, ny)
    up = (lax.rem(ix + 1, nx), iy, ih)
    down = (lax.rem(ix + nx - 1, nx), iy, ih)
    barrier = pltpu.get_barrier_semaphore()
    for device in (up, down):
        pl.semaphore_signal(barrier, inc=1, device_id=device, device_id_type=MESH)

    def copy_of(i, plane, side, device):
        return pltpu.make_async_remote_copy(
            src_ref=mid_ref.at[plane], dst_ref=side_ref.at[side], send_sem=send_sems.at[i], recv_sem=recv_sems.at[i],
            device_id=device, device_id_type=MESH,
        )

    to_up = copy_of(0, 1, 0, up)
    to_down = copy_of(1, 0, 1, down)

    def exchange():
        pl.semaphore_wait(barrier, 2)
        to_up.start()
        to_down.start()


    @pl.when(late > 1)
    def _():
        exchange()

    acc_c[...] = acc_c_in[...]
    acc_d[...] = acc_d_in[...]

    def tile_of(X, Y, Z):
        return mid_ref[X - 1, Y, Z] if X in (1, 2) else side_ref[X // 3, Y, Z]

    target, targets, prep, reduce_pairs, flat, phase = machinery(
        tile_of, a_ref, q_ref, b_ref, cc, cd, sqb, acc_c, acc_d
    )
    targets()
    for new in (bins_mid(0, 3, 0), bins_mid(0, 3, 2)):
        prep(new)
    reduce_pairs(phase(pair_y_near, 8, NONE))

    @pl.when(late > 0)
    def _():
        prep(bins_mid(1, 1, 2))
        reduce_pairs(phase(pair_mid_far, 8, NONE))

    @pl.when(late == 1)
    def _():
        exchange()

    last = phase(pair_y_far, 4, NONE)
    to_down.wait_recv()
    prep(bins_side(1, 0))
    prep(bins_side(1, 2))
    last = phase(pair_x_near(1), 6, last, following=pair_x_far(1))
    last = phase(pair_x_far(1), 3, last, opening=False)

    @pl.when(late == 0)
    def _():
        exchange()


    to_up.wait_recv()
    prep(bins_side(0, 0))
    prep(bins_side(0, 2))
    last = phase(pair_x_near(0), 6, last, following=pair_x_far(0))
    last = phase(pair_x_far(0), 3, last, opening=False)
    reduce_pairs(last)

    for o in range(8):
        tile, x, y, z = target(o)
        tp = [x, y, z]
        cv = acc_c[o, 8:11] + acc_c[o, 0:3]
        dq = (acc_d[o, 32:48] + acc_d[o, 16:32]) + acc_d[o, 0:16]
        live = tile[3:4] * NORM
        xf = (x * dq[0:1] + y * dq[1:2] + z * dq[2:3]) - dq[3:4]
        for a in range(3):
            i = 4 + 4 * a
            v = cv[a:a + 1] + tp[a] * xf
            v = v - ((x * dq[i:i + 1] + y * dq[i + 1:i + 2] + z * dq[i + 2:i + 3]) - dq[i + 3:i + 4])
            out_ref[a, o:o + 1] = v * live
    to_up.wait_send()
    to_down.wait_send()


WORK = [
    pltpu.VMEM((64, 128, 32), BF16),
    pltpu.VMEM((65, 64, 128), BF16),
    pltpu.VMEM((8, 32, 512), BF16),
    pltpu.VMEM((4, 256, 128), BF16),
    pltpu.VMEM((4, 256, 128), BF16),
    pltpu.VMEM((4, 128, 512), F32),
]
NONE = [(64, 0)] * 4
SUMS = [(8, 16, 128), (8, 48, 128)]


def on_device(offsets, forces, counts):
    vmem = pl.BlockSpec(memory_space=pltpu.VMEM)
    mid, sum_c, sum_d = pl.pallas_call(
        own_kernel,
        out_shape=[jax.ShapeDtypeStruct(s, F32) for s in [(2, 4, 4, 8, 128)] + SUMS],
        in_specs=[vmem, vmem, pl.BlockSpec(memory_space=pltpu.SMEM)],
        out_specs=[vmem] * 3,
        scratch_shapes=[pltpu.VMEM((2, 2, 2, 8, 128), F32)] + WORK + [pltpu.SemaphoreType.DMA((12,))] * 2,
        compiler_params=pltpu.CompilerParams(collective_id=0, has_side_effects=True),
    )(offsets.reshape(3, 8, 128), forces.reshape(3, 8, 128), counts)
    vel = pl.pallas_call(
        near_kernel,
        out_shape=jax.ShapeDtypeStruct((3, 8, 128), F32),
        in_specs=[vmem] * 3,
        out_specs=vmem,
        scratch_shapes=[pltpu.VMEM((2, 4, 4, 8, 128), F32)] + [pltpu.VMEM(s, F32) for s in SUMS] + WORK
        + [pltpu.SemaphoreType.DMA((2,))] * 2,
        compiler_params=pltpu.CompilerParams(collective_id=1, has_side_effects=True),
    )(mid, sum_c, sum_d)
    return vel.reshape(3, 2, 2, 2, 128)


def solution(mesh):
    spec = P(None, "gx", "gy", "ha", None)
    return jax.shard_map(
        on_device, mesh=mesh, in_specs=(spec, spec, P("gx", "gy", "ha")), out_specs=spec, check_vma=False
    )
```

```python
import math

import jax
import jax.numpy as jnp
from jax import lax
from jax.experimental import pallas as pl
from jax.experimental.pallas import tpu as pltpu
from jax.sharding import PartitionSpec as P


GAUSS = 4.0 / math.sqrt(math.pi)
NORM = 1.0 / (8.0 * math.pi)
ERFCX = (-6.605853591129529e-05, 0.2835500330769051, 0.2685154202156198, 0.31675806246707194,
         -0.03963002369445217, 0.48597127806071433, -0.4204782835714706, 0.1053890269858883)
F32 = jnp.float32
BF16 = jnp.bfloat16
MESH = pl.DeviceIdType.MESH
FORMS = ((1.0, 0.0), (8.0 * GAUSS, -3.0 * GAUSS), (8.0 * GAUSS, -GAUSS), (-4.0 * math.log2(math.e), 0.0))


def split3(v):
    a = v.astype(BF16).astype(F32)
    r = v - a
    b = r.astype(BF16).astype(F32)
    return a, b, r - b


def coefs(sq, ac, ad, arg, keep=None):
    rs = lax.rsqrt(sq)
    z = sq * rs + 1.0
    t = lax.rsqrt(z * z)
    p = ERFCX[7]
    for q in ERFCX[6::-1]:
        p = p * t + q
    e = rs * p
    g = jnp.exp2(arg)
    if keep is not None:
        g = jnp.where(keep, g, 0.0)
    c = g * (e + ac)
    d = (g * (rs * rs)) * (e - ad)
    ch = c.astype(BF16)
    cl = (c - ch.astype(F32)).astype(BF16)
    dh = d.astype(BF16)
    dl = (d - dh.astype(F32)).astype(BF16)
    return ch, cl, dh, dl


def odd(i):
    return i - 2 * lax.shift_right_logical(i, 1)


def pair_own(i, k):
    return 16 + 16 * odd(i) + (1 + k // 2) * 4 + k % 2, lax.shift_right_logical(i, 1)


def pair_y_near(i, k):
    return (1 + k // 2) * 16 + 12 * odd(lax.shift_right_logical(i, 1)) + k % 2, i


def pair_mid_far(i, k):
    return (1 + k // 2) * 16 + (1 + k % 2) * 4 + 3 - odd(i), i


def pair_y_far(i, k):
    return (1 + k % 2) * 16 + 12 * odd(i) + 3 - k // 2, 2 * i + k // 2


def pair_x_near(side):
    def pair(i, k):
        y = lax.shift_right_logical(11 * i, 5)
        return 48 * side + (i - 2 * y) * 4 + k % 2, 4 * side + 2 * y + k // 2
    return pair


def pair_x_far(side):
    def pair(i, k):
        return 48 * side + (k // 2 + i) * 4 + 3 - k % 2, jnp.int32(0) + 4 * side + k
    return pair


def bins_mid(y0, ystep, z0):
    def new(n):
        return 1 + n // 4, y0 + ystep * ((n // 2) % 2), z0 + n % 2
    return new


def bins_side(side, z0):
    def new(n):
        return 3 * side, n // 2, z0 + n % 2
    return new


def machinery(tile_of, a_ref, q_ref, b_ref, cc, cd, sqb, acc_c, acc_d):
    sub = lax.broadcasted_iota(jnp.int32, (128, 128), 0)
    diff = lax.broadcasted_iota(jnp.int32, (128, 128), 1) - sub
    one = jnp.ones((1, 128), F32)
    zero = jnp.zeros((1, 128), F32)
    cc[...] = jnp.zeros((4, 256, 128), F32).astype(BF16)
    cd[...] = jnp.zeros((4, 256, 128), F32).astype(BF16)
    q_ref[64] = jnp.zeros((64, 128), F32).astype(BF16)

    def target(o):
        tile = tile_of(1 + o // 4, 1 + (o // 2) % 2, o % 2)
        x = tile[4:5] + float(o // 4 - 1)
        y = tile[5:6] + float((o // 2) % 2 - 1)
        z = tile[6:7] + float(o % 2 - 1)
        return tile, x, y, z

    def targets():
        for o in range(8):
            tile, x, y, z = target(o)
            m = x * x + y * y + z * z + 0.01
            for k, (scale, extra) in enumerate(FORMS):
                t1, t2, t3 = split3(scale * jnp.concatenate([x, y, z, one], axis=0))
                m1, m2, m3 = split3(scale * m + extra)
                b_ref[o, :, 128 * k:128 * (k + 1)] = jnp.concatenate(
                    [t1, t2, t3, t1, t2, t1, m1, m2, m3, zero, zero, zero, zero, zero], axis=0
                ).astype(BF16)

    def prep(new):
        for k in range(8):
            X, Y, Z = new(k)
            b = X * 16 + Y * 4 + Z
            tile = tile_of(X, Y, Z)
            f = tile[0:3]
            x = tile[4:5] + float(X - 2)
            y = tile[5:6] + float(Y - 2)
            z = tile[6:7] + float(Z - 1 - 4 * (Z // 3))
            n = x * x + y * y + z * z
            r1, r2, r3 = split3(jnp.concatenate([-2.0 * x, -2.0 * y, -2.0 * z, n], axis=0))
            feat = jnp.concatenate([r1, r1, r1, r2, r2, r3, jnp.ones((8, 128), F32)], axis=0)
            a_ref[b] = feat.T.astype(BF16)
            w = x * f[0:1] + y * f[1:2] + z * f[2:3]
            g4 = jnp.concatenate([f, w], axis=0)
            a3 = split3(jnp.concatenate([g4, x * g4], axis=0))
            b3 = split3(jnp.concatenate([y * g4, z * g4], axis=0))
            q = jnp.concatenate([a3[0], a3[1], a3[0], b3[0], a3[1], b3[1], a3[2], b3[2]], axis=0)
            q_ref[b] = q.astype(BF16)

    def reduce_pairs(pairs, first=0):
        for k, (b, o) in enumerate(pairs, first):
            q = q_ref[b]
            q2 = jnp.concatenate([q, q], axis=1)
            acc_c[o] = acc_c[o] + jnp.dot(q2[0:16], cc[k], preferred_element_type=F32)
            acc_d[o] = acc_d[o] + jnp.dot(q2[16:64], cd[k], preferred_element_type=F32)

    def distances(pairs, first=0):
        for k, (b, o) in enumerate(pairs, first):
            sqb[k] = jnp.dot(a_ref[b], b_ref[o], preferred_element_type=F32)

    def flat(pair, i):
        return [pair(jnp.asarray(i, jnp.int32), k) for k in range(4)]

    def phase(pair, n, last, mask=False, opening=True, following=None, start=0):
        if opening:
            distances(flat(pair, start))

        @pl.loop(0, n)
        def _(i):
            began = lax.div(i + n - 1, n)
            now = flat(pair, start + i - began)
            pending = [(pb + began * (b - pb), po + began * (o - po)) for (b, o), (pb, po) in zip(now, last)]
            ended = lax.div(i + 1, n)
            later = flat(pair, start + i + 1 - ended)
            if following is not None:
                first = flat(following, 0)
                later = [(b + ended * (nb - b), o + ended * (no - o)) for (b, o), (nb, no) in zip(later, first)]
            for k in range(4):
                keep = None
                if mask:
                    off = 4 * odd(start + i) + k - lax.shift_right_logical(start + i, 1)
                    keep = diff != off * off * 1000
                v = sqb[k]
                ch, cl, dh, dl = coefs(v[:, 0:128], v[:, 128:256], v[:, 256:384], v[:, 384:512], keep)
                distances([later[k]], k)
                reduce_pairs([pending[k]], k)
                cc[k, 0:128] = ch
                cc[k, 128:256] = cl
                cd[k, 0:128] = dh
                cd[k, 128:256] = dl

        return flat(pair, start + n - 1)

    return target, targets, prep, reduce_pairs, flat, phase


def lateness(ix, iy, ny):
    return lax.rem(ix, 8) * 2 + lax.div(ny - iy, ny)


def own_kernel(off_ref, frc_ref, cnt_ref, mid_ref, acc_c, acc_d, send_ref, a_ref, q_ref, b_ref, cc, cd, sqb, send_sems, recv_sems):
    ix = lax.axis_index("gx")
    iy = lax.axis_index("gy")
    ih = lax.axis_index("ha")
    ny = lax.axis_size("gy")
    partner = (ix, iy, 1 - ih)
    beside = {dy: (ix, lax.rem(iy + dy + ny, ny), ih) for dy in (1, -1)}
    barrier = pltpu.get_barrier_semaphore()
    for device in (partner, beside[1], beside[-1]):
        pl.semaphore_signal(barrier, inc=1, device_id=device, device_id_type=MESH)

    lane = lax.broadcasted_iota(jnp.int32, (1, 128), 1)
    for b in range(8):
        bx, by, bz = b // 4, (b // 2) % 2, b % 2
        live = (lane < cnt_ref[bx, by, bz]).astype(F32)
        rows = [frc_ref[r, b:b + 1] * live for r in range(3)] + [live]
        rows += [off_ref[r, b:b + 1] for r in range(3)] + [jnp.zeros((1, 128), F32)]
        tile = jnp.concatenate(rows, axis=0)
        send_ref[bx, by, bz] = tile
        mid_ref[bx, 1 + by, bz] = tile
    acc_c[...] = jnp.zeros_like(acc_c)
    acc_d[...] = jnp.zeros_like(acc_d)
    target, targets, prep, reduce_pairs, flat, phase = machinery(
        lambda X, Y, Z: mid_ref[X - 1, Y, Z], a_ref, q_ref, b_ref, cc, cd, sqb, acc_c, acc_d
    )
    copies = []

    def send(src, dst, device):
        i = len(copies)
        copy = pltpu.make_async_remote_copy(
            src_ref=src, dst_ref=dst, send_sem=send_sems.at[i], recv_sem=recv_sems.at[i],
            device_id=device, device_id_type=MESH,
        )
        copy.start()
        copies.append(copy)

    targets()
    prep(bins_mid(1, 1, 0))
    late = lateness(ix, iy, ny)

    @pl.when(late == 0)
    def _():
        reduce_pairs(phase(pair_own, 16, NONE, mask=True))

    pl.semaphore_wait(barrier, 3)
    columns = [(sx, sy) for sx in range(2) for sy in range(2)]
    for sx, sy in columns:
        send(send_ref.at[sx, sy], mid_ref.at[sx, 1 + sy, pl.ds(2, 2)], partner)
    for dy in (1, -1):
        for sx in range(2):
            send(send_ref.at[sx, (1 + dy) // 2], mid_ref.at[sx, (3 - 3 * dy) // 2, pl.ds(0, 2)], beside[dy])

    @pl.when(late > 0)
    def _():
        reduce_pairs(phase(pair_own, 10, NONE, mask=True))

    for i, (sx, sy) in enumerate(columns):
        copies[i].wait_recv()
        dy = 2 * sy - 1
        send(mid_ref.at[sx, 1 + sy, pl.ds(2, 2)], mid_ref.at[sx, (3 - 3 * dy) // 2, pl.ds(2, 2)], beside[dy])

    @pl.when(late > 0)
    def _():
        reduce_pairs(phase(pair_own, 6, NONE, mask=True, start=10))

    @pl.when(late == 0)
    def _():
        prep(bins_mid(1, 1, 2))
        reduce_pairs(phase(pair_mid_far, 8, NONE))

    for copy in copies[4:]:
        copy.wait_recv()
    for copy in copies:
        copy.wait_send()


def near_kernel(mid_ref, acc_c_in, acc_d_in, out_ref, side_ref, acc_c, acc_d, a_ref, q_ref, b_ref, cc, cd, sqb, send_sems, recv_sems):
    ix = lax.axis_index("gx")
    iy = lax.axis_index("gy")
    ih = lax.axis_index("ha")
    nx = lax.axis_size("gx")
    ny = lax.axis_size("gy")
    late = lateness(ix, iy, ny)
    up = (lax.rem(ix + 1, nx), iy, ih)
    down = (lax.rem(ix + nx - 1, nx), iy, ih)
    barrier = pltpu.get_barrier_semaphore()
    for device in (up, down):
        pl.semaphore_signal(barrier, inc=1, device_id=device, device_id_type=MESH)

    def copy_of(i, plane, side, device):
        return pltpu.make_async_remote_copy(
            src_ref=mid_ref.at[plane], dst_ref=side_ref.at[side], send_sem=send_sems.at[i], recv_sem=recv_sems.at[i],
            device_id=device, device_id_type=MESH,
        )

    to_up = copy_of(0, 1, 0, up)
    to_down = copy_of(1, 0, 1, down)

    def exchange():
        pl.semaphore_wait(barrier, 2)
        to_up.start()
        to_down.start()


    @pl.when(late > 1)
    def _():
        exchange()

    acc_c[...] = acc_c_in[...]
    acc_d[...] = acc_d_in[...]

    def tile_of(X, Y, Z):
        return mid_ref[X - 1, Y, Z] if X in (1, 2) else side_ref[X // 3, Y, Z]

    target, targets, prep, reduce_pairs, flat, phase = machinery(
        tile_of, a_ref, q_ref, b_ref, cc, cd, sqb, acc_c, acc_d
    )
    targets()
    for new in (bins_mid(0, 3, 0), bins_mid(0, 3, 2)):
        prep(new)
    reduce_pairs(phase(pair_y_near, 8, NONE))

    @pl.when(late > 0)
    def _():
        prep(bins_mid(1, 1, 2))
        reduce_pairs(phase(pair_mid_far, 8, NONE))

    @pl.when(late == 1)
    def _():
        exchange()

    last = phase(pair_y_far, 4, NONE)
    to_down.wait_recv()
    prep(bins_side(1, 0))
    prep(bins_side(1, 2))
    last = phase(pair_x_near(1), 6, last, following=pair_x_far(1))
    last = phase(pair_x_far(1), 3, last, opening=False)

    @pl.when(late == 0)
    def _():
        exchange()


    to_up.wait_recv()
    prep(bins_side(0, 0))
    prep(bins_side(0, 2))
    last = phase(pair_x_near(0), 6, last, following=pair_x_far(0))
    last = phase(pair_x_far(0), 3, last, opening=False)
    reduce_pairs(last)

    for o in range(8):
        tile, x, y, z = target(o)
        tp = [x, y, z]
        cv = acc_c[o, 8:11] + acc_c[o, 0:3]
        dq = (acc_d[o, 32:48] + acc_d[o, 16:32]) + acc_d[o, 0:16]
        live = tile[3:4]
        xf = (x * dq[0:1] + y * dq[1:2] + z * dq[2:3]) - dq[3:4]
        for a in range(3):
            i = 4 + 4 * a
            v = cv[a:a + 1] + tp[a] * xf
            v = v - ((x * dq[i:i + 1] + y * dq[i + 1:i + 2] + z * dq[i + 2:i + 3]) - dq[i + 3:i + 4])
            out_ref[a, o:o + 1] = v * live
    to_up.wait_send()
    to_down.wait_send()


WORK = [
    pltpu.VMEM((64, 128, 32), BF16),
    pltpu.VMEM((65, 64, 128), BF16),
    pltpu.VMEM((8, 32, 512), BF16),
    pltpu.VMEM((4, 256, 128), BF16),
    pltpu.VMEM((4, 256, 128), BF16),
    pltpu.VMEM((4, 128, 512), F32),
]
NONE = [(64, 0)] * 4
SUMS = [(8, 16, 128), (8, 48, 128)]


def on_device(offsets, forces, counts):
    vmem = pl.BlockSpec(memory_space=pltpu.VMEM)
    mid, sum_c, sum_d = pl.pallas_call(
        own_kernel,
        out_shape=[jax.ShapeDtypeStruct(s, F32) for s in [(2, 4, 4, 8, 128)] + SUMS],
        in_specs=[vmem, vmem, pl.BlockSpec(memory_space=pltpu.SMEM)],
        out_specs=[vmem] * 3,
        scratch_shapes=[pltpu.VMEM((2, 2, 2, 8, 128), F32)] + WORK + [pltpu.SemaphoreType.DMA((12,))] * 2,
        compiler_params=pltpu.CompilerParams(collective_id=0, has_side_effects=True),
    )(offsets.reshape(3, 8, 128), forces.reshape(3, 8, 128), counts)
    vel = pl.pallas_call(
        near_kernel,
        out_shape=jax.ShapeDtypeStruct((3, 8, 128), F32),
        in_specs=[vmem] * 3,
        out_specs=vmem,
        scratch_shapes=[pltpu.VMEM((2, 4, 4, 8, 128), F32)] + [pltpu.VMEM(s, F32) for s in SUMS] + WORK
        + [pltpu.SemaphoreType.DMA((2,))] * 2,
        compiler_params=pltpu.CompilerParams(collective_id=1, has_side_effects=True),
    )(mid, sum_c, sum_d)
    return vel.reshape(3, 2, 2, 2, 128) * NORM


def solution(mesh):
    spec = P(None, "gx", "gy", "ha", None)
    return jax.shard_map(
        on_device, mesh=mesh, in_specs=(spec, spec, P("gx", "gy", "ha")), out_specs=spec, check_vma=False
    )
```
